32 devices in a mesh: groups: 2 (over x), seq: 16 (over z, y, core).
Axes of the slice: x: 2, y: 2, z: 4, core: 2. Of those that a mesh axis runs over, the one named last changes fastest.
Arguments:
- tokens: bfloat16 [4096, 1536], P(('groups', 'seq')), parts along dimension 0, as said below
- held_block: int32 [32], P('groups'), parts along dimension 0, may hold values from 0 to 15, each once
- lengths: int32 [6], P('groups'), parts along dimension 0, may hold values from 2 to 8, as said below
- shift: float32 [6, 1536], P('groups'), parts along dimension 0, may hold values from -5 to 5
- scale: float32 [6, 1536], P('groups'), parts along dimension 0, as said below
- gate: float32 [6, 1536], P('groups'), parts along dimension 0, may hold values from -5 to 5
- w_qkv: bfloat16 [1536, 2304], replicated, as said below
- w_out: bfloat16 [768, 1536], replicated, may hold values from -0.21875 to 0.21875
Outputs:
- update: bfloat16 [4096, 1536], P(('groups', 'seq')), parts along dimension 0
The draws below stay inside these ranges and needn't reach their ends.
There are 2 independent parts, one for each index of `groups`. The reference program is written for one: setup_inputs(seed, part) draws one part's arguments, and reference() takes and returns one part's arrays. A program takes and returns all parts, laid end to end along the dimension named above; an argument that names none is the same for every part. Nothing has to cross between parts.
Inputs may be any that keep to these rules, and one draw needn't show every extreme that they name: `held_block`: each device holds a different block. The lengths sum to 16; the first video is the longest, with exactly 8 blocks. `tokens`: finite values. `scale`: finite values. `w_qkv`: finite values.
All inputs are finite; a program needn't handle non-finite values.
Results may differ from the reference program's by a relative error of at most 0.0078.
Values may be sent and summed in bfloat16 or wider, within the bound.
A program may use at most 128 MiB of HBM per device.

```python
import math
import jax
import jax.numpy as jnp
from jax import lax

D = 1536
HEADS = 6
HSIZE = 128
NVID = 3
HD = 768
TOKENS = 2048
N_SEQ = 16


def draw_lengths(key, part):
    second = N_SEQ // 3 + jax.random.randint(key, (), -(N_SEQ // 16), N_SEQ // 16 + 1)
    first = jnp.asarray(N_SEQ // 2, jnp.int32)
    third = N_SEQ - first - second
    return jnp.stack([first, second, third]).astype(jnp.int32)


def draw_tokens(key, part):
    keys = jax.random.split(key, 3)
    columns = jnp.exp(jax.random.uniform(keys[1], (1, D)) * math.log(10.0))
    rowscale = jnp.exp(jax.random.uniform(keys[2], (TOKENS, 1)) * math.log(10.0))
    base = jax.random.normal(keys[0], (TOKENS, D)) * columns * rowscale
    return (0.3 * base).astype(jnp.bfloat16)


def draw_scale(key, part):
    values = 0.5 * jax.random.normal(key, (NVID, D))
    return values.astype(jnp.float32)


def draw_w_qkv(key, part):
    keys = jax.random.split(key, 1)
    factor = 1.0 / math.sqrt(D)
    base = factor * jax.random.normal(keys[0], (D, 3 * HD))
    return base.astype(jnp.bfloat16)


def bell_draw(key, extent, deviation, limit, kind=jnp.bfloat16):
    return jnp.clip(deviation * jax.random.normal(key, extent, jnp.float32), -limit, limit).astype(kind)


def setup_inputs(seed: int = 0, part: int = 0) -> dict:
    arg_keys = jax.random.split(jax.random.key(seed), 9)
    own_keys = jax.random.split(jax.random.fold_in(arg_keys[8], part), 9)
    return {
        "tokens": draw_tokens(jax.random.fold_in(jax.random.fold_in(arg_keys[8], part), 71), part),
        "held_block": jax.random.permutation(own_keys[1], N_SEQ).astype(jnp.int32),
        "lengths": draw_lengths(jax.random.fold_in(jax.random.fold_in(arg_keys[8], part), 71), part),
        "shift": bell_draw(own_keys[3], (NVID, D), 1.0, 5.0, jnp.float32),
        "scale": draw_scale(jax.random.fold_in(jax.random.fold_in(arg_keys[8], part), 71), part),
        "gate": bell_draw(own_keys[5], (NVID, D), 1.0, 5.0, jnp.float32),
        "w_qkv": draw_w_qkv(jax.random.fold_in(arg_keys[8], 71), part),
        "w_out": bell_draw(arg_keys[7], (HD, D), HD ** -0.5, 0.21875),
    }


def reference(tokens, held_block, lengths, shift, scale, gate, w_qkv, w_out):
    ndev = held_block.shape[0]
    rows = tokens.shape[0] // ndev
    ends = jnp.cumsum(lengths).astype(jnp.int32)
    block_ids = jnp.arange(ndev, dtype=jnp.int32)
    block_video = lax.optimization_barrier(jnp.sum((block_ids[:, None] >= ends[None, :]).astype(jnp.int32), axis=1)).astype(jnp.int32)
    dev_video = block_video[held_block]
    values_in = tokens.reshape(ndev, rows, D).astype(jnp.float32)
    mean = lax.optimization_barrier(jnp.mean(values_in, axis=2, keepdims=True))
    var = lax.optimization_barrier(jnp.mean((values_in - mean) ** 2, axis=2, keepdims=True))
    normed = (values_in - mean) * lax.rsqrt(var + 1e-06)
    normed = normed * (1.0 + scale[dev_video][:, None, :]) + shift[dev_video][:, None, :]
    normed = normed.astype(jnp.bfloat16).reshape(ndev * rows, D)
    qkv = jnp.dot(normed, w_qkv, preferred_element_type=jnp.float32).astype(jnp.bfloat16)
    holder = jnp.zeros((ndev,), jnp.int32).at[held_block].set(block_ids)
    packed = qkv.reshape(ndev, rows, 3 * HD)[holder].reshape(ndev * rows, 3 * HD)
    seg = jnp.repeat(block_video, rows)
    query = packed[:, :HD].reshape(-1, HEADS, HSIZE).astype(jnp.float32)
    keys = packed[:, HD:2 * HD].reshape(-1, HEADS, HSIZE).astype(jnp.float32)
    vals = packed[:, 2 * HD:].reshape(-1, HEADS, HSIZE).astype(jnp.float32)
    tile = math.gcd(TOKENS, 512)
    inv = 1.0 / math.sqrt(HSIZE)

    def tile_attend(index):
        start = (index * tile).astype(jnp.int32)
        rows_q = lax.dynamic_slice_in_dim(query, start, tile, 0)
        seg_q = lax.dynamic_slice_in_dim(seg, start, tile, 0)
        scores = jnp.einsum('qhd,khd->hqk', rows_q, keys) * inv
        mask = (seg_q[:, None] == seg[None, :])[None, :, :]
        scores = jnp.where(mask, scores, -1e+30)
        top = lax.optimization_barrier(jnp.max(scores, axis=2, keepdims=True))
        weight = jnp.where(mask, jnp.exp(scores - top), 0.0)
        total = lax.optimization_barrier(jnp.sum(weight, axis=2))
        weight16 = weight.astype(jnp.bfloat16).astype(jnp.float32)
        summed = jnp.einsum('hqk,khd->qhd', weight16, vals)
        return (summed / jnp.transpose(total)[:, :, None]).astype(jnp.bfloat16)
    attended = lax.map(tile_attend, jnp.arange(TOKENS // tile, dtype=jnp.int32))
    attended = attended.reshape(ndev, rows, HD)[held_block].reshape(ndev * rows, HD)
    mixed = jnp.dot(attended, w_out, preferred_element_type=jnp.float32)
    mixed = mixed * jnp.repeat(gate[dev_video], rows, axis=0)
    return mixed.astype(jnp.bfloat16)
```

```python
import functools
import math

import jax
import jax.numpy as jnp
from jax import lax
from jax.experimental import pallas as pl
from jax.experimental.pallas import tpu as pltpu
from jax.sharding import PartitionSpec as P

HEADS = 6
HSIZE = 128
MESH = pl.DeviceIdType.MESH
NEG = -math.inf
LIMIT = 24


def spread(
    count,
    held_hbm,
    len_hbm,
    tok_hbm,
    shift_hbm,
    scale_hbm,
    gate_hbm,
    w_hbm,
    att_out,
    gate_out,
    held_ref,
    len_ref,
    tok_ref,
    shift_ref,
    scale_ref,
    gate_ref,
    wkv_vm,
    wq_vm,
    norm_vm,
    tkv,
    tq,
    rkv,
    rq,
    ao,
    att,
    holder,
    in_sem,
    w_sem,
    wq_sem,
    tkv_sem,
    rkv_sem,
    tq_sem,
    rq_sem,
    fwd_sem,
    ao_sem,
    att_sem,
):
    rows, _ = tok_ref.shape
    nvid = len_ref.shape[0]
    pairs = count // 2
    me = lax.axis_index("seq")
    layers = count // 4
    z = me // 4
    y = lax.rem(me // 2, 2)
    core = lax.rem(me, 2)
    low_half = z < layers // 2
    edge = jnp.logical_or(z == 0, z == layers - 1)
    active = jnp.logical_or(jnp.logical_not(edge), core == 0)
    my_head = jnp.where(edge, jnp.where(z == 0, 0, HEADS - 1), 2 * z - 1 + y)
    partner = jnp.where(edge, z * 4 + (1 - y) * 2 + core, z * 4 + y * 2 + 1 - core)
    half = HEADS // 2

    barrier = pltpu.get_barrier_semaphore()

    def greet(i, _):
        d = lax.rem(me + i, count)
        pl.semaphore_signal(barrier, inc=1, device_id={"seq": d}, device_id_type=MESH)
        return 0

    lax.fori_loop(1, count, greet, 0, unroll=5)

    def head_at(i):
        first = jnp.where(low_half, half, 0)
        return lax.rem(i // half * half + first, HEADS) + lax.rem(i + z + y + core, half)

    def load_w(h, part):
        return pltpu.make_async_copy(
            w_hbm.at[:, pl.ds(pl.multiple_of(((part + 1) * HEADS + h) * HSIZE, HSIZE), HSIZE)],
            wkv_vm.at[h, :, pl.ds(part * HSIZE, HSIZE)],
            w_sem.at[h, part],
        )

    loads = [
        pltpu.make_async_copy(src, dst, in_sem.at[i])
        for i, (src, dst) in enumerate(
            (
                (tok_hbm, tok_ref),
                (held_hbm, held_ref),
                (len_hbm, len_ref),
                (shift_hbm, shift_ref),
                (scale_hbm, scale_ref),
                (gate_hbm, gate_ref),
            )
        )
    ]
    for load in loads:
        load.start()
    for i in range(HEADS):
        for part in range(2):
            load_w(head_at(i), part).start()
    load_q = pltpu.make_async_copy(w_hbm.at[:, 0 : HEADS * HSIZE], wq_vm, wq_sem)
    load_q.start()

    def span(block):
        video = jnp.int32(0)
        start = jnp.int32(0)
        end = len_ref[0]
        run = len_ref[0]
        for v in range(1, nvid):
            nxt = run + len_ref[v]
            inside = block >= run
            video = jnp.where(inside, v, video)
            start = jnp.where(inside, run, start)
            end = jnp.where(inside, nxt, end)
            run = nxt
        return video, start, end

    for load in loads:
        load.wait()
    my_video, _, _ = span(held_ref[me])

    x = tok_ref[...].astype(jnp.float32)
    mean = jnp.mean(x, axis=1, keepdims=True)
    x = x - mean
    var = jnp.mean(x * x, axis=1, keepdims=True)
    x = x * lax.rsqrt(var + 1e-6)
    x = x * (1.0 + scale_ref[pl.ds(my_video, 1), :]) + shift_ref[pl.ds(my_video, 1), :]
    norm_vm[...] = x.astype(jnp.bfloat16)

    def target(h):
        side = jnp.where(h == 0, y * 2, (layers - 1) * 4 + y * 2)
        return jnp.where(jnp.logical_or(h == 0, h == HEADS - 1), side, (h + 1) * 2 + core)

    def ship(h, src, dst, send, recv):
        return pltpu.make_async_remote_copy(
            src_ref=src.at[h],
            dst_ref=dst.at[me],
            send_sem=send.at[h],
            recv_sem=recv.at[me],
            device_id={"seq": target(h)},
            device_id_type=MESH,
        )

    def dispatch(h, src, dst, send, recv):
        dest = target(h)

        @pl.when(dest == me)
        def _():
            pltpu.make_async_copy(src.at[h], dst.at[me], recv.at[me]).start()

        @pl.when(dest != me)
        def _():
            ship(h, src, dst, send, recv).start()

    def project(i):
        h = head_at(i)
        for part in range(2):
            load_w(h, part).wait()
        tkv[h] = jnp.dot(norm_vm[...], wkv_vm[h], preferred_element_type=jnp.float32).astype(
            jnp.bfloat16
        )

    def send_kv(i, _):
        project(i)
        dispatch(head_at(i), tkv, rkv, tkv_sem, rkv_sem)
        return 0

    project(0)
    pl.semaphore_wait(barrier, count - 1)
    dispatch(head_at(0), tkv, rkv, tkv_sem, rkv_sem)
    lax.fori_loop(1, HEADS, send_kv, 0)

    load_q.wait()
    queries = jnp.dot(norm_vm[...], wq_vm[...], preferred_element_type=jnp.float32).astype(
        jnp.bfloat16
    )
    for h in range(HEADS):
        tq[h] = queries[:, h * HSIZE : (h + 1) * HSIZE]

    def send_q(i, _):
        dispatch(head_at(i), tq, rq, tq_sem, rq_sem)
        return 0

    lax.fori_loop(0, HEADS, send_q, 0)

    gate_out[...] = gate_ref[pl.ds(my_video, 1), :]

    def find(b, _):
        def look(d, acc):
            return jnp.where(held_ref[d] == b, d, acc)

        holder[b] = lax.fori_loop(0, count, look, jnp.int32(0), unroll=16)
        return 0

    lax.fori_loop(0, count, find, 0)

    near = jnp.where(low_half, 0, pairs // 2)

    def mine(t):
        return jnp.where(edge, t // 2 * 4 + y * 2 + lax.rem(t, 2), t * 2 + core)

    def other(t):
        return jnp.where(edge, t // 2 * 4 + (1 - y) * 2 + lax.rem(t, 2), t * 2 + 1 - core)

    def forward(t):
        s = mine(t)
        return pltpu.make_async_remote_copy(
            src_ref=rkv.at[s],
            dst_ref=rkv.at[s],
            send_sem=fwd_sem.at[t],
            recv_sem=rkv_sem.at[s],
            device_id={"seq": partner},
            device_id_type=MESH,
        )

    chunk = count // 2
    inv = math.log2(math.e) / math.sqrt(HSIZE)

    def back(t):
        s = mine(t)
        return s, pltpu.make_async_remote_copy(
            src_ref=ao.at[t],
            dst_ref=att.at[my_head],
            send_sem=ao_sem.at[t],
            recv_sem=att_sem.at[my_head],
            device_id={"seq": s},
            device_id_type=MESH,
        )

    @pl.when(active)
    def _():
        def relay(i, _):
            t = lax.rem(i + near, pairs)
            s = mine(t)
            pltpu.make_async_copy(rkv.at[s], rkv.at[s], rkv_sem.at[s]).wait()
            forward(t).start()
            return 0

        lax.fori_loop(0, pairs, relay, 0)

        def gather(i, _):
            s = other(lax.rem(i + near, pairs))
            pltpu.make_async_copy(rkv.at[s], rkv.at[s], rkv_sem.at[s]).wait()
            return 0

        lax.fori_loop(0, pairs, gather, 0)

        def attend(t):
            s = mine(t)
            _, start, end = span(held_ref[s])
            query = rq[s]
            scores = []
            where = []
            for j in range(chunk):
                block = start + j
                slot = holder[jnp.maximum(jnp.minimum(block, end - 1), 0)]
                where.append(slot)
                score = lax.dot_general(
                    query,
                    rkv[slot, :, 0:HSIZE],
                    (((1,), (1,)), ((), ())),
                    preferred_element_type=jnp.float32,
                )
                scores.append(score + jnp.where(block < end, 0.0, NEG))
            high = functools.reduce(jnp.maximum, scores)
            top = jnp.max(high, axis=1, keepdims=True)
            sums = None
            summed = None
            for j in range(chunk):
                weight = jnp.exp2((scores[j] - top) * inv)
                sums = weight if sums is None else sums + weight
                term = jnp.dot(
                    weight.astype(jnp.bfloat16),
                    rkv[where[j], :, HSIZE : 2 * HSIZE],
                    preferred_element_type=jnp.float32,
                )
                summed = term if summed is None else summed + term
            total = jnp.sum(sums, axis=1, keepdims=True)
            return (summed / total).astype(jnp.bfloat16)

        def answer(i, _):
            some = [lax.rem(near + pairs // 2, pairs) + i, near + i]
            for t in some:
                s = mine(t)
                pltpu.make_async_copy(rq.at[s], rq.at[s], rq_sem.at[s]).wait()
            for t, value in zip(some, [attend(t) for t in some]):
                s, copy = back(t)
                ao[t] = value

                @pl.when(s == me)
                def _():
                    pltpu.make_async_copy(ao.at[t], att.at[my_head], att_sem.at[my_head]).start()

                @pl.when(s != me)
                def _():
                    copy.start()

            return 0

        lax.fori_loop(0, pairs // 2, answer, 0)

    for h in range(HEADS):
        pltpu.make_async_copy(att.at[h], att.at[h], att_sem.at[h]).wait()
        att_out[:, h * HSIZE : (h + 1) * HSIZE] = att[h]

    def drain(h, _):
        @pl.when(target(h) != me)
        def _():
            ship(h, tkv, rkv, tkv_sem, rkv_sem).wait_send()
            ship(h, tq, rq, tq_sem, rq_sem).wait_send()

        return 0

    lax.fori_loop(0, HEADS, drain, 0)

    @pl.when(active)
    def _():
        def drain_back(t, _):
            forward(t).wait_send()
            s, copy = back(t)

            @pl.when(s != me)
            def _():
                copy.wait_send()

            return 0

        lax.fori_loop(0, pairs, drain_back, 0)


def finish(att_ref, gate_ref, wo_ref, out_ref):
    mixed = jnp.dot(att_ref[...], wo_ref[...], preferred_element_type=jnp.float32)
    out_ref[...] = (mixed * gate_ref[...]).astype(out_ref.dtype)


def small(tokens, held_block, lengths, shift, scale, gate, w_qkv, w_out):
    count = lax.axis_size("seq")
    rows, width = tokens.shape
    pairs = count // 2
    wide = HEADS * HSIZE
    vmem = pl.BlockSpec(memory_space=pltpu.VMEM)
    hbm = pl.BlockSpec(memory_space=pltpu.HBM)
    dma = pltpu.SemaphoreType.DMA
    half = jnp.bfloat16
    pinned = [
        pltpu.with_memory_space_constraint(x, pltpu.HBM)
        for x in (held_block, lengths, tokens, shift, scale, gate, w_qkv)
    ]
    attended, row = pl.pallas_call(
        functools.partial(spread, count),
        out_shape=(
            jax.ShapeDtypeStruct((rows, wide), half),
            jax.ShapeDtypeStruct((1, width), jnp.float32),
        ),
        in_specs=[hbm] * 7,
        out_specs=(vmem, vmem),
        scratch_shapes=[
            pltpu.SMEM(held_block.shape, jnp.int32),
            pltpu.SMEM(lengths.shape, jnp.int32),
            pltpu.VMEM(tokens.shape, tokens.dtype),
            pltpu.VMEM(shift.shape, jnp.float32),
            pltpu.VMEM(scale.shape, jnp.float32),
            pltpu.VMEM(gate.shape, jnp.float32),
            pltpu.VMEM((HEADS, width, 2 * HSIZE), half),
            pltpu.VMEM((width, wide), half),
            pltpu.VMEM((rows, width), half),
            pltpu.VMEM((HEADS, rows, 2 * HSIZE), half),
            pltpu.VMEM((HEADS, rows, HSIZE), half),
            pltpu.VMEM((count, rows, 2 * HSIZE), half),
            pltpu.VMEM((count, rows, HSIZE), half),
            pltpu.VMEM((pairs, rows, HSIZE), half),
            pltpu.VMEM((HEADS, rows, HSIZE), half),
            pltpu.SMEM((count,), jnp.int32),
            dma((6,)),
            dma((HEADS, 2)),
            dma,
            dma((HEADS,)),
            dma((count,)),
            dma((HEADS,)),
            dma((count,)),
            dma((pairs,)),
            dma((pairs,)),
            dma((HEADS,)),
        ],
        compiler_params=pltpu.CompilerParams(
            collective_id=1, has_side_effects=True, vmem_limit_bytes=LIMIT * 1024 * 1024
        ),
    )(*pinned)
    return pl.pallas_call(
        finish,
        out_shape=jax.ShapeDtypeStruct((rows, width), half),
        in_specs=[vmem] * 3,
        out_specs=vmem,
        compiler_params=pltpu.CompilerParams(vmem_limit_bytes=LIMIT * 1024 * 1024),
    )(attended, row, w_out)


def kernel(
    count,
    held_hbm,
    len_hbm,
    tok_hbm,
    shift_hbm,
    scale_hbm,
    gate_hbm,
    w_hbm,
    wo_hbm,
    out_ref,
    held_ref,
    len_ref,
    tok_ref,
    shift_ref,
    scale_ref,
    gate_ref,
    w_vm,
    wo_vm,
    norm_vm,
    tx,
    rx,
    ao,
    att,
    total_ref,
    holder,
    in_sem,
    w_sem,
    wo_sem,
    tx_sem,
    rx_sem,
    fwd_sem,
    ao_sem,
    att_sem,
):
    rows, _ = tok_ref.shape
    nvid = len_ref.shape[0]
    pairs = count // 2
    teams = pairs // HEADS
    shift = (pairs - teams * HEADS) // 2
    me = lax.axis_index("seq")
    chip = me // 2
    core = lax.rem(me, 2)
    sibling = chip * 2 + 1 - core

    barrier = pltpu.get_barrier_semaphore()

    def greet(i, _):
        d = lax.rem(chip + i, pairs) * 2 + core
        pl.semaphore_signal(barrier, inc=1, device_id={"seq": d}, device_id_type=MESH)
        return 0

    lax.fori_loop(1, pairs, greet, 0, unroll=7)
    pl.semaphore_signal(barrier, inc=1, device_id={"seq": sibling}, device_id_type=MESH)

    low_half = chip < pairs // 2

    def head_at(i):
        first = jnp.where(low_half, HEADS // 2, 0) if teams == 1 else 0
        part = HEADS // 2
        return lax.rem(i // part * part + first, HEADS) + lax.rem(i + chip // 2 + chip, part)

    def load_w(h, part):
        return pltpu.make_async_copy(
            w_hbm.at[:, pl.ds(pl.multiple_of((part * HEADS + h) * HSIZE, HSIZE), HSIZE)],
            w_vm.at[h, :, pl.ds(part * HSIZE, HSIZE)],
            w_sem.at[h, part],
        )

    loads = [
        pltpu.make_async_copy(src, dst, in_sem.at[i])
        for i, (src, dst) in enumerate(
            (
                (tok_hbm, tok_ref),
                (held_hbm, held_ref),
                (len_hbm, len_ref),
                (shift_hbm, shift_ref),
                (scale_hbm, scale_ref),
                (gate_hbm, gate_ref),
            )
        )
    ]
    for load in loads:
        load.start()
    for i in range(HEADS // 2):
        for part in range(3):
            load_w(head_at(i), part).start()
    load_wo = pltpu.make_async_copy(wo_hbm, wo_vm, wo_sem)

    def span(block):
        video = jnp.int32(0)
        start = jnp.int32(0)
        end = len_ref[0]
        run = len_ref[0]
        for v in range(1, nvid):
            nxt = run + len_ref[v]
            inside = block >= run
            video = jnp.where(inside, v, video)
            start = jnp.where(inside, run, start)
            end = jnp.where(inside, nxt, end)
            run = nxt
        return video, start, end

    for load in loads:
        load.wait()
    my_video, _, _ = span(held_ref[me])

    x = tok_ref[...].astype(jnp.float32)
    mean = jnp.mean(x, axis=1, keepdims=True)
    x = x - mean
    var = jnp.mean(x * x, axis=1, keepdims=True)
    x = x * lax.rsqrt(var + 1e-6)
    x = x * (1.0 + scale_ref[pl.ds(my_video, 1), :]) + shift_ref[pl.ds(my_video, 1), :]
    norm_vm[...] = x.astype(jnp.bfloat16)

    for i in range(HEADS // 2, HEADS):
        for part in range(3):
            load_w(head_at(i), part).start()
    pl.semaphore_wait(barrier, pairs)

    def ship(h, team):
        dest = (team * HEADS + h + shift) * 2 + core
        return dest, pltpu.make_async_remote_copy(
            src_ref=tx.at[h],
            dst_ref=rx.at[me],
            send_sem=tx_sem.at[h, team],
            recv_sem=rx_sem.at[me],
            device_id={"seq": dest},
            device_id_type=MESH,
        )

    def project(i, _):
        h = head_at(i)
        for part in range(3):
            load_w(h, part).wait()
        tx[h] = jnp.dot(norm_vm[...], w_vm[h], preferred_element_type=jnp.float32).astype(
            jnp.bfloat16
        )

        def send(team, _):
            dest, copy = ship(h, team)

            @pl.when(dest == me)
            def _():
                pltpu.make_async_copy(tx.at[h], rx.at[me], rx_sem.at[me]).start()

            @pl.when(dest != me)
            def _():
                copy.start()

            return 0

        lax.fori_loop(0, teams, send, 0)
        return 0

    lax.fori_loop(0, HEADS, project, 0)

    load_wo.start()

    def find(b, _):
        def look(d, acc):
            return jnp.where(held_ref[d] == b, d, acc)

        holder[b] = lax.fori_loop(0, count, look, jnp.int32(0), unroll=16)
        return 0

    lax.fori_loop(0, count, find, 0)

    active = jnp.logical_and(chip >= shift, chip < teams * HEADS + shift)
    place = jnp.where(active, chip - shift, 0)
    my_head = lax.rem(place, HEADS)
    my_team = place // HEADS
    near = jnp.where(low_half, 0, pairs // 2)
    kv_cols = pl.ds(HSIZE, 2 * HSIZE)

    def forward(s):
        return pltpu.make_async_remote_copy(
            src_ref=rx.at[s, :, kv_cols],
            dst_ref=rx.at[s, :, kv_cols],
            send_sem=fwd_sem.at[s // 2],
            recv_sem=rx_sem.at[s],
            device_id={"seq": sibling},
            device_id_type=MESH,
        )

    key_blocks = count // 2
    chunk = min(8, key_blocks)
    turns = key_blocks // chunk
    mine = pairs if teams == 1 else (pairs - my_team + teams - 1) // teams
    width = 2 if teams == 1 and pairs % 2 == 0 else 1
    inv = math.log2(math.e) / math.sqrt(HSIZE)

    def back(t):
        s = (my_team + t * teams) * 2 + core
        return s, pltpu.make_async_remote_copy(
            src_ref=ao.at[t],
            dst_ref=att.at[my_head],
            send_sem=ao_sem.at[t],
            recv_sem=att_sem.at[my_head],
            device_id={"seq": s},
            device_id_type=MESH,
        )

    @pl.when(active)
    def _():
        def relay(i, _):
            s = lax.rem(i + near, pairs) * 2 + core
            pltpu.make_async_copy(rx.at[s], rx.at[s], rx_sem.at[s]).wait()
            forward(s).start()
            return 0

        lax.fori_loop(0, pairs, relay, 0)

        def gather(i, _):
            s = lax.rem(i + near, pairs) * 2 + 1 - core
            part = rx.at[s, :, kv_cols]
            pltpu.make_async_copy(part, part, rx_sem.at[s]).wait()
            return 0

        lax.fori_loop(0, pairs, gather, 0)

        def attend(t):
            s, _ = back(t)
            _, start, end = span(held_ref[s])
            query = rx[s, :, 0:HSIZE]

            def key_turn(turn, carry):
                top, total, summed = carry
                scores = []
                where = []
                for j in range(chunk):
                    block = start + turn * chunk + j
                    slot = holder[jnp.maximum(jnp.minimum(block, end - 1), 0)]
                    where.append(slot)
                    score = lax.dot_general(
                        query,
                        rx[slot, :, HSIZE : 2 * HSIZE],
                        (((1,), (1,)), ((), ())),
                        preferred_element_type=jnp.float32,
                    )
                    bias = jnp.where(block < end, 0.0, NEG)
                    scores.append(score + bias)
                high = functools.reduce(jnp.maximum, scores)
                new_top = jnp.maximum(top, jnp.max(high, axis=1, keepdims=True))
                factor = jnp.exp2((top - new_top) * inv)
                total = total * factor
                summed = summed * factor
                sums = None
                for j in range(chunk):
                    weight = jnp.exp2((scores[j] - new_top) * inv)
                    sums = weight if sums is None else sums + weight
                    summed = summed + jnp.dot(
                        weight.astype(jnp.bfloat16),
                        rx[where[j], :, 2 * HSIZE : 3 * HSIZE],
                        preferred_element_type=jnp.float32,
                    )
                total = total + jnp.sum(sums, axis=1, keepdims=True)
                return new_top, total, summed

            carry = (
                jnp.full((rows, 1), NEG, jnp.float32),
                jnp.zeros((rows, 1), jnp.float32),
                jnp.zeros((rows, HSIZE), jnp.float32),
            )
            if turns == 1:
                carry = key_turn(0, carry)
            else:
                carry = lax.fori_loop(0, turns, key_turn, carry)
            _, total, summed = carry
            return (summed / total).astype(jnp.bfloat16)

        def answer(i, _):
            some = [
                lax.rem(i * width + u + jnp.where(low_half, mine // 2, 0), mine)
                for u in range(width)
            ]
            for t, value in zip(some, [attend(t) for t in some]):
                s, copy = back(t)
                ao[t] = value

                @pl.when(s == me)
                def _():
                    pltpu.make_async_copy(ao.at[t], att.at[my_head], att_sem.at[my_head]).start()

                @pl.when(s != me)
                def _():
                    copy.start()

            return 0

        lax.fori_loop(0, mine // width, answer, 0)

    load_wo.wait()
    part = HEADS // 2
    first = jnp.where(low_half, 0, part) if teams == 1 else 0

    def mix(first):
        for h in range(part):
            pltpu.make_async_copy(att.at[first + h], att.at[first + h], att_sem.at[first + h]).wait()
        attended = jnp.concatenate([att[first + h] for h in range(part)], axis=1)
        weights = wo_vm[pl.ds(pl.multiple_of(first * HSIZE, HSIZE), part * HSIZE), :]
        return jnp.dot(attended, weights, preferred_element_type=jnp.float32)

    total_ref[...] = mix(first)
    mixed = total_ref[...] + mix(part - first)
    out_ref[...] = (mixed * gate_ref[pl.ds(my_video, 1), :]).astype(out_ref.dtype)

    def drain(i, _):
        h = lax.rem(i, HEADS)
        dest, copy = ship(h, i // HEADS)

        @pl.when(dest != me)
        def _():
            copy.wait_send()

        return 0

    lax.fori_loop(0, HEADS * teams, drain, 0)

    @pl.when(active)
    def _():
        def drain_forward(i, _):
            forward(i * 2 + core).wait_send()
            return 0

        lax.fori_loop(0, pairs, drain_forward, 0)

        def drain_back(t, _):
            s, copy = back(t)

            @pl.when(s != me)
            def _():
                copy.wait_send()

            return 0

        lax.fori_loop(0, mine, drain_back, 0)


def large(tokens, held_block, lengths, shift, scale, gate, w_qkv, w_out):
    count = lax.axis_size("seq")
    rows, width = tokens.shape
    pairs = count // 2
    teams = pairs // HEADS
    slots = -(-pairs // teams)
    vmem = pl.BlockSpec(memory_space=pltpu.VMEM)
    hbm = pl.BlockSpec(memory_space=pltpu.HBM)
    dma = pltpu.SemaphoreType.DMA
    return pl.pallas_call(
        functools.partial(kernel, count),
        out_shape=jax.ShapeDtypeStruct((rows, width), jnp.bfloat16),
        in_specs=[hbm] * 8,
        out_specs=vmem,
        scratch_shapes=[
            pltpu.SMEM(held_block.shape, jnp.int32),
            pltpu.SMEM(lengths.shape, jnp.int32),
            pltpu.VMEM(tokens.shape, tokens.dtype),
            pltpu.VMEM(shift.shape, jnp.float32),
            pltpu.VMEM(scale.shape, jnp.float32),
            pltpu.VMEM(gate.shape, jnp.float32),
            pltpu.VMEM((HEADS, width, 3 * HSIZE), jnp.bfloat16),
            pltpu.VMEM(w_out.shape, jnp.bfloat16),
            pltpu.VMEM((rows, width), jnp.bfloat16),
            pltpu.VMEM((HEADS, rows, 3 * HSIZE), jnp.bfloat16),
            pltpu.VMEM((count, rows, 3 * HSIZE), jnp.bfloat16),
            pltpu.VMEM((slots, rows, HSIZE), jnp.bfloat16),
            pltpu.VMEM((HEADS, rows, HSIZE), jnp.bfloat16),
            pltpu.VMEM((rows, width), jnp.float32),
            pltpu.SMEM((count,), jnp.int32),
            dma((6,)),
            dma((HEADS, 3)),
            dma,
            dma((HEADS, teams)),
            dma((count,)),
            dma((pairs,)),
            dma((slots,)),
            dma((HEADS,)),
        ],
        compiler_params=pltpu.CompilerParams(
            collective_id=0, has_side_effects=True, vmem_limit_bytes=61 * 1024 * 1024
        ),
    )(held_block, lengths, tokens, shift, scale, gate, w_qkv, w_out)


def shards(*args):
    return small(*args) if lax.axis_size("seq") == 16 else large(*args)


def solution(mesh):
    placed = (
        P(("groups", "seq"), None),
        P("groups"),
        P("groups"),
        P("groups", None),
        P("groups", None),
        P("groups", None),
        P(),
        P(),
    )
    return jax.shard_map(
        shards, mesh=mesh, in_specs=placed, out_specs=P(("groups", "seq"), None), check_vma=False
    )
```

```python
import functools
import math

import jax
import jax.numpy as jnp
from jax import lax
from jax.experimental import pallas as pl
from jax.experimental.pallas import tpu as pltpu
from jax.sharding import PartitionSpec as P

HEADS = 6
HSIZE = 128
MESH = pl.DeviceIdType.MESH
NEG = -math.inf
LIMIT = 24


def spread(
    count,
    held_hbm,
    len_hbm,
    tok_hbm,
    shift_hbm,
    scale_hbm,
    gate_hbm,
    w_hbm,
    att_out,
    gate_out,
    held_ref,
    len_ref,
    tok_ref,
    shift_ref,
    scale_ref,
    gate_ref,
    wkv_vm,
    wq_vm,
    norm_vm,
    tkv,
    tq,
    rkv,
    rq,
    ao,
    att,
    holder,
    in_sem,
    w_sem,
    wq_sem,
    tkv_sem,
    rkv_sem,
    tq_sem,
    rq_sem,
    fwd_sem,
    ao_sem,
    att_sem,
):
    rows, _ = tok_ref.shape
    nvid = len_ref.shape[0]
    pairs = count // 2
    me = lax.axis_index("seq")
    layers = count // 4
    z = me // 4
    y = lax.rem(me // 2, 2)
    core = lax.rem(me, 2)
    low_half = z < layers // 2
    chip = me // 2
    active = jnp.logical_and(chip >= 1, chip <= HEADS)
    my_head = jnp.where(active, chip - 1, 0)
    sibling = chip * 2 + 1 - core
    half = HEADS // 2

    barrier = pltpu.get_barrier_semaphore()

    def greet(i, _):
        d = lax.rem(me + i, count)
        pl.semaphore_signal(barrier, inc=1, device_id={"seq": d}, device_id_type=MESH)
        return 0

    lax.fori_loop(1, count, greet, 0, unroll=5)

    def head_at(i):
        upper = lax.rem(i // half + jnp.where(low_half, 1, 0), 2)
        k = lax.rem(i, half)
        middle = upper * (half - 1) + 1 + lax.rem(k + y + core, half - 1)
        return jnp.where(k == 0, upper * (HEADS - 1), middle)

    def load_w(h, part):
        return pltpu.make_async_copy(
            w_hbm.at[:, pl.ds(pl.multiple_of(((part + 1) * HEADS + h) * HSIZE, HSIZE), HSIZE)],
            wkv_vm.at[h, :, pl.ds(part * HSIZE, HSIZE)],
            w_sem.at[h, part],
        )

    loads = [
        pltpu.make_async_copy(src, dst, in_sem.at[i])
        for i, (src, dst) in enumerate(
            (
                (tok_hbm, tok_ref),
                (held_hbm, held_ref),
                (len_hbm, len_ref),
                (shift_hbm, shift_ref),
                (scale_hbm, scale_ref),
                (gate_hbm, gate_ref),
            )
        )
    ]
    for load in loads:
        load.start()
    for i in range(HEADS):
        for part in range(2):
            load_w(head_at(i), part).start()
    load_q = pltpu.make_async_copy(w_hbm.at[:, 0 : HEADS * HSIZE], wq_vm, wq_sem)
    load_q.start()

    def span(block):
        video = jnp.int32(0)
        start = jnp.int32(0)
        end = len_ref[0]
        run = len_ref[0]
        for v in range(1, nvid):
            nxt = run + len_ref[v]
            inside = block >= run
            video = jnp.where(inside, v, video)
            start = jnp.where(inside, run, start)
            end = jnp.where(inside, nxt, end)
            run = nxt
        return video, start, end

    for load in loads:
        load.wait()
    my_video, _, _ = span(held_ref[me])

    x = tok_ref[...].astype(jnp.float32)
    mean = jnp.mean(x, axis=1, keepdims=True)
    x = x - mean
    var = jnp.mean(x * x, axis=1, keepdims=True)
    x = x * lax.rsqrt(var + 1e-6)
    x = x * (1.0 + scale_ref[pl.ds(my_video, 1), :]) + shift_ref[pl.ds(my_video, 1), :]
    norm_vm[...] = x.astype(jnp.bfloat16)

    def target(h):
        return (h + 1) * 2 + core

    def ship(h, src, dst, send, recv):
        return pltpu.make_async_remote_copy(
            src_ref=src.at[h],
            dst_ref=dst.at[me],
            send_sem=send.at[h],
            recv_sem=recv.at[me],
            device_id={"seq": target(h)},
            device_id_type=MESH,
        )

    def dispatch(h, src, dst, send, recv):
        dest = target(h)

        @pl.when(dest == me)
        def _():
            pltpu.make_async_copy(src.at[h], dst.at[me], recv.at[me]).start()

        @pl.when(dest != me)
        def _():
            ship(h, src, dst, send, recv).start()

    def project(i):
        h = head_at(i)
        for part in range(2):
            load_w(h, part).wait()
        tkv[h] = jnp.dot(norm_vm[...], wkv_vm[h], preferred_element_type=jnp.float32).astype(
            jnp.bfloat16
        )

    def send_kv(i, _):
        project(i)
        dispatch(head_at(i), tkv, rkv, tkv_sem, rkv_sem)
        return 0

    project(0)
    pl.semaphore_wait(barrier, count - 1)
    dispatch(head_at(0), tkv, rkv, tkv_sem, rkv_sem)
    lax.fori_loop(1, HEADS, send_kv, 0)

    load_q.wait()
    queries = jnp.dot(norm_vm[...], wq_vm[...], preferred_element_type=jnp.float32).astype(
        jnp.bfloat16
    )
    for h in range(HEADS):
        tq[h] = queries[:, h * HSIZE : (h + 1) * HSIZE]

    def send_q(i, _):
        dispatch(head_at(i), tq, rq, tq_sem, rq_sem)
        return 0

    lax.fori_loop(0, HEADS, send_q, 0)

    gate_out[...] = gate_ref[pl.ds(my_video, 1), :]

    def find(b, _):
        def look(d, acc):
            return jnp.where(held_ref[d] == b, d, acc)

        holder[b] = lax.fori_loop(0, count, look, jnp.int32(0), unroll=16)
        return 0

    lax.fori_loop(0, count, find, 0)

    def order(i):
        return jnp.where(low_half, pairs - 1 - i, i)

    def forward(t):
        s = t * 2 + core
        return pltpu.make_async_remote_copy(
            src_ref=rkv.at[s],
            dst_ref=rkv.at[s],
            send_sem=fwd_sem.at[t],
            recv_sem=rkv_sem.at[s],
            device_id={"seq": sibling},
            device_id_type=MESH,
        )

    chunk = count // 2
    inv = math.log2(math.e) / math.sqrt(HSIZE)

    def back(t):
        s = t * 2 + core
        return s, pltpu.make_async_remote_copy(
            src_ref=ao.at[t],
            dst_ref=att.at[my_head],
            send_sem=ao_sem.at[t],
            recv_sem=att_sem.at[my_head],
            device_id={"seq": s},
            device_id_type=MESH,
        )

    @pl.when(active)
    def _():
        def relay(i, _):
            t = order(lax.rem(i + pairs // 2, pairs))
            s = t * 2 + core
            pltpu.make_async_copy(rkv.at[s], rkv.at[s], rkv_sem.at[s]).wait()
            forward(t).start()
            return 0

        lax.fori_loop(0, pairs, relay, 0)

        def gather(i, _):
            s = order(lax.rem(i + pairs // 2, pairs)) * 2 + 1 - core
            pltpu.make_async_copy(rkv.at[s], rkv.at[s], rkv_sem.at[s]).wait()
            return 0

        lax.fori_loop(0, pairs, gather, 0)

        def attend(t):
            s = t * 2 + core
            _, start, end = span(held_ref[s])
            query = rq[s]
            slots = [
                holder[jnp.maximum(jnp.minimum(start + j, end - 1), 0)] for j in range(chunk)
            ]
            keys = jnp.concatenate([rkv[slot, :, 0:HSIZE] for slot in slots], axis=0)
            values = jnp.concatenate([rkv[slot, :, HSIZE : 2 * HSIZE] for slot in slots], axis=0)
            scores = lax.dot_general(
                query, keys, (((1,), (1,)), ((), ())), preferred_element_type=jnp.float32
            )
            scores = [scores[:, j * HSIZE : (j + 1) * HSIZE] for j in range(chunk)]
            top = jnp.max(functools.reduce(jnp.maximum, scores), axis=1, keepdims=True)
            weights = [
                jnp.exp2((scores[j] - jnp.where(start + j < end, top, math.inf)) * inv)
                for j in range(chunk)
            ]
            total = jnp.sum(functools.reduce(jnp.add, weights), axis=1, keepdims=True)
            weight16 = jnp.concatenate([weight.astype(jnp.bfloat16) for weight in weights], axis=1)
            summed = jnp.dot(weight16, values, preferred_element_type=jnp.float32)
            return (summed / total).astype(jnp.bfloat16)

        def answer(i, _):
            some = [order(i), jnp.where(low_half, 0, pairs // 2) + i]
            for t in some:
                s = t * 2 + core
                pltpu.make_async_copy(rq.at[s], rq.at[s], rq_sem.at[s]).wait()
            for t, value in zip(some, [attend(t) for t in some]):
                s, copy = back(t)
                ao[t] = value

                @pl.when(s == me)
                def _():
                    pltpu.make_async_copy(ao.at[t], att.at[my_head], att_sem.at[my_head]).start()

                @pl.when(s != me)
                def _():
                    copy.start()

            return 0

        lax.fori_loop(0, pairs // 2, answer, 0)

    for h in range(HEADS):
        pltpu.make_async_copy(att.at[h], att.at[h], att_sem.at[h]).wait()
        att_out[:, h * HSIZE : (h + 1) * HSIZE] = att[h]

    def drain(h, _):
        @pl.when(target(h) != me)
        def _():
            ship(h, tkv, rkv, tkv_sem, rkv_sem).wait_send()
            ship(h, tq, rq, tq_sem, rq_sem).wait_send()

        return 0

    lax.fori_loop(0, HEADS, drain, 0)

    @pl.when(active)
    def _():
        def drain_back(t, _):
            forward(t).wait_send()
            s, copy = back(t)

            @pl.when(s != me)
            def _():
                copy.wait_send()

            return 0

        lax.fori_loop(0, pairs, drain_back, 0)


def finish(att_ref, gate_ref, wo_ref, out_ref):
    mixed = jnp.dot(att_ref[...], wo_ref[...], preferred_element_type=jnp.float32)
    out_ref[...] = (mixed * gate_ref[...]).astype(out_ref.dtype)


def small(tokens, held_block, lengths, shift, scale, gate, w_qkv, w_out):
    count = lax.axis_size("seq")
    rows, width = tokens.shape
    pairs = count // 2
    wide = HEADS * HSIZE
    vmem = pl.BlockSpec(memory_space=pltpu.VMEM)
    hbm = pl.BlockSpec(memory_space=pltpu.HBM)
    dma = pltpu.SemaphoreType.DMA
    half = jnp.bfloat16
    pinned = [
        pltpu.with_memory_space_constraint(x, pltpu.HBM)
        for x in (held_block, lengths, tokens, shift, scale, gate, w_qkv)
    ]
    attended, row = pl.pallas_call(
        functools.partial(spread, count),
        out_shape=(
            jax.ShapeDtypeStruct((rows, wide), half),
            jax.ShapeDtypeStruct((1, width), jnp.float32),
        ),
        in_specs=[hbm] * 7,
        out_specs=(vmem, vmem),
        scratch_shapes=[
            pltpu.SMEM(held_block.shape, jnp.int32),
            pltpu.SMEM(lengths.shape, jnp.int32),
            pltpu.VMEM(tokens.shape, tokens.dtype),
            pltpu.VMEM(shift.shape, jnp.float32),
            pltpu.VMEM(scale.shape, jnp.float32),
            pltpu.VMEM(gate.shape, jnp.float32),
            pltpu.VMEM((HEADS, width, 2 * HSIZE), half),
            pltpu.VMEM((width, wide), half),
            pltpu.VMEM((rows, width), half),
            pltpu.VMEM((HEADS, rows, 2 * HSIZE), half),
            pltpu.VMEM((HEADS, rows, HSIZE), half),
            pltpu.VMEM((count, rows, 2 * HSIZE), half),
            pltpu.VMEM((count, rows, HSIZE), half),
            pltpu.VMEM((pairs, rows, HSIZE), half),
            pltpu.VMEM((HEADS, rows, HSIZE), half),
            pltpu.SMEM((count,), jnp.int32),
            dma((6,)),
            dma((HEADS, 2)),
            dma,
            dma((HEADS,)),
            dma((count,)),
            dma((HEADS,)),
            dma((count,)),
            dma((pairs,)),
            dma((pairs,)),
            dma((HEADS,)),
        ],
        compiler_params=pltpu.CompilerParams(
            collective_id=1, has_side_effects=True, vmem_limit_bytes=LIMIT * 1024 * 1024
        ),
    )(*pinned)
    return pl.pallas_call(
        finish,
        out_shape=jax.ShapeDtypeStruct((rows, width), half),
        in_specs=[vmem] * 3,
        out_specs=vmem,
        compiler_params=pltpu.CompilerParams(vmem_limit_bytes=LIMIT * 1024 * 1024),
    )(attended, row, w_out)


def kernel(
    count,
    held_hbm,
    len_hbm,
    tok_hbm,
    shift_hbm,
    scale_hbm,
    gate_hbm,
    w_hbm,
    wo_hbm,
    out_ref,
    held_ref,
    len_ref,
    tok_ref,
    shift_ref,
    scale_ref,
    gate_ref,
    w_vm,
    wo_vm,
    norm_vm,
    tx,
    rx,
    ao,
    att,
    total_ref,
    holder,
    in_sem,
    w_sem,
    wo_sem,
    tx_sem,
    rx_sem,
    fwd_sem,
    ao_sem,
    att_sem,
):
    rows, _ = tok_ref.shape
    nvid = len_ref.shape[0]
    pairs = count // 2
    teams = pairs // HEADS
    shift = (pairs - teams * HEADS) // 2
    me = lax.axis_index("seq")
    chip = me // 2
    core = lax.rem(me, 2)
    sibling = chip * 2 + 1 - core

    barrier = pltpu.get_barrier_semaphore()

    def greet(i, _):
        d = lax.rem(chip + i, pairs) * 2 + core
        pl.semaphore_signal(barrier, inc=1, device_id={"seq": d}, device_id_type=MESH)
        return 0

    lax.fori_loop(1, pairs, greet, 0, unroll=7)
    pl.semaphore_signal(barrier, inc=1, device_id={"seq": sibling}, device_id_type=MESH)

    low_half = chip < pairs // 2

    def head_at(i):
        first = jnp.where(low_half, HEADS // 2, 0) if teams == 1 else 0
        part = HEADS // 2
        return lax.rem(i // part * part + first, HEADS) + lax.rem(i + chip // 2 + chip, part)

    def load_w(h, part):
        return pltpu.make_async_copy(
            w_hbm.at[:, pl.ds(pl.multiple_of((part * HEADS + h) * HSIZE, HSIZE), HSIZE)],
            w_vm.at[h, :, pl.ds(part * HSIZE, HSIZE)],
            w_sem.at[h, part],
        )

    loads = [
        pltpu.make_async_copy(src, dst, in_sem.at[i])
        for i, (src, dst) in enumerate(
            (
                (tok_hbm, tok_ref),
                (held_hbm, held_ref),
                (len_hbm, len_ref),
                (shift_hbm, shift_ref),
                (scale_hbm, scale_ref),
                (gate_hbm, gate_ref),
            )
        )
    ]
    for load in loads:
        load.start()
    for i in range(HEADS // 2):
        for part in range(3):
            load_w(head_at(i), part).start()
    load_wo = pltpu.make_async_copy(wo_hbm, wo_vm, wo_sem)

    def span(block):
        video = jnp.int32(0)
        start = jnp.int32(0)
        end = len_ref[0]
        run = len_ref[0]
        for v in range(1, nvid):
            nxt = run + len_ref[v]
            inside = block >= run
            video = jnp.where(inside, v, video)
            start = jnp.where(inside, run, start)
            end = jnp.where(inside, nxt, end)
            run = nxt
        return video, start, end

    for load in loads:
        load.wait()
    my_video, _, _ = span(held_ref[me])

    x = tok_ref[...].astype(jnp.float32)
    mean = jnp.mean(x, axis=1, keepdims=True)
    x = x - mean
    var = jnp.mean(x * x, axis=1, keepdims=True)
    x = x * lax.rsqrt(var + 1e-6)
    x = x * (1.0 + scale_ref[pl.ds(my_video, 1), :]) + shift_ref[pl.ds(my_video, 1), :]
    norm_vm[...] = x.astype(jnp.bfloat16)

    for i in range(HEADS // 2, HEADS):
        for part in range(3):
            load_w(head_at(i), part).start()
    pl.semaphore_wait(barrier, pairs)

    def ship(h, team):
        dest = (team * HEADS + h + shift) * 2 + core
        return dest, pltpu.make_async_remote_copy(
            src_ref=tx.at[h],
            dst_ref=rx.at[me],
            send_sem=tx_sem.at[h, team],
            recv_sem=rx_sem.at[me],
            device_id={"seq": dest},
            device_id_type=MESH,
        )

    def project(i, _):
        h = head_at(i)
        for part in range(3):
            load_w(h, part).wait()
        tx[h] = jnp.dot(norm_vm[...], w_vm[h], preferred_element_type=jnp.float32).astype(
            jnp.bfloat16
        )

        def send(team, _):
            dest, copy = ship(h, team)

            @pl.when(dest == me)
            def _():
                pltpu.make_async_copy(tx.at[h], rx.at[me], rx_sem.at[me]).start()

            @pl.when(dest != me)
            def _():
                copy.start()

            return 0

        lax.fori_loop(0, teams, send, 0)
        return 0

    lax.fori_loop(0, HEADS, project, 0)

    load_wo.start()

    def find(b, _):
        def look(d, acc):
            return jnp.where(held_ref[d] == b, d, acc)

        holder[b] = lax.fori_loop(0, count, look, jnp.int32(0), unroll=16)
        return 0

    lax.fori_loop(0, count, find, 0)

    active = jnp.logical_and(chip >= shift, chip < teams * HEADS + shift)
    place = jnp.where(active, chip - shift, 0)
    my_head = lax.rem(place, HEADS)
    my_team = place // HEADS
    near = jnp.where(low_half, 0, pairs // 2)
    kv_cols = pl.ds(HSIZE, 2 * HSIZE)

    def forward(s):
        return pltpu.make_async_remote_copy(
            src_ref=rx.at[s, :, kv_cols],
            dst_ref=rx.at[s, :, kv_cols],
            send_sem=fwd_sem.at[s // 2],
            recv_sem=rx_sem.at[s],
            device_id={"seq": sibling},
            device_id_type=MESH,
        )

    key_blocks = count // 2
    chunk = min(8, key_blocks)
    turns = key_blocks // chunk
    mine = pairs if teams == 1 else (pairs - my_team + teams - 1) // teams
    width = 2 if teams == 1 and pairs % 2 == 0 else 1
    inv = math.log2(math.e) / math.sqrt(HSIZE)

    def back(t):
        s = (my_team + t * teams) * 2 + core
        return s, pltpu.make_async_remote_copy(
            src_ref=ao.at[t],
            dst_ref=att.at[my_head],
            send_sem=ao_sem.at[t],
            recv_sem=att_sem.at[my_head],
            device_id={"seq": s},
            device_id_type=MESH,
        )

    @pl.when(active)
    def _():
        def relay(i, _):
            s = lax.rem(i + near, pairs) * 2 + core
            pltpu.make_async_copy(rx.at[s], rx.at[s], rx_sem.at[s]).wait()
            forward(s).start()
            return 0

        lax.fori_loop(0, pairs, relay, 0)

        def gather(i, _):
            s = lax.rem(i + near, pairs) * 2 + 1 - core
            part = rx.at[s, :, kv_cols]
            pltpu.make_async_copy(part, part, rx_sem.at[s]).wait()
            return 0

        lax.fori_loop(0, pairs, gather, 0)

        def attend(t):
            s, _ = back(t)
            _, start, end = span(held_ref[s])
            query = rx[s, :, 0:HSIZE]

            def key_turn(turn, carry):
                top, total, summed = carry
                scores = []
                where = []
                for j in range(chunk):
                    block = start + turn * chunk + j
                    slot = holder[jnp.maximum(jnp.minimum(block, end - 1), 0)]
                    where.append(slot)
                    score = lax.dot_general(
                        query,
                        rx[slot, :, HSIZE : 2 * HSIZE],
                        (((1,), (1,)), ((), ())),
                        preferred_element_type=jnp.float32,
                    )
                    bias = jnp.where(block < end, 0.0, NEG)
                    scores.append(score + bias)
                high = functools.reduce(jnp.maximum, scores)
                new_top = jnp.maximum(top, jnp.max(high, axis=1, keepdims=True))
                factor = jnp.exp2((top - new_top) * inv)
                total = total * factor
                summed = summed * factor
                sums = None
                for j in range(chunk):
                    weight = jnp.exp2((scores[j] - new_top) * inv)
                    sums = weight if sums is None else sums + weight
                    summed = summed + jnp.dot(
                        weight.astype(jnp.bfloat16),
                        rx[where[j], :, 2 * HSIZE : 3 * HSIZE],
                        preferred_element_type=jnp.float32,
                    )
                total = total + jnp.sum(sums, axis=1, keepdims=True)
                return new_top, total, summed

            carry = (
                jnp.full((rows, 1), NEG, jnp.float32),
                jnp.zeros((rows, 1), jnp.float32),
                jnp.zeros((rows, HSIZE), jnp.float32),
            )
            if turns == 1:
                carry = key_turn(0, carry)
            else:
                carry = lax.fori_loop(0, turns, key_turn, carry)
            _, total, summed = carry
            return (summed / total).astype(jnp.bfloat16)

        def answer(i, _):
            some = [
                lax.rem(i * width + u + jnp.where(low_half, mine // 2, 0), mine)
                for u in range(width)
            ]
            for t, value in zip(some, [attend(t) for t in some]):
                s, copy = back(t)
                ao[t] = value

                @pl.when(s == me)
                def _():
                    pltpu.make_async_copy(ao.at[t], att.at[my_head], att_sem.at[my_head]).start()

                @pl.when(s != me)
                def _():
                    copy.start()

            return 0

        lax.fori_loop(0, mine // width, answer, 0)

    load_wo.wait()
    part = HEADS // 2
    first = jnp.where(low_half, 0, part) if teams == 1 else 0

    def mix(first):
        for h in range(part):
            pltpu.make_async_copy(att.at[first + h], att.at[first + h], att_sem.at[first + h]).wait()
        attended = jnp.concatenate([att[first + h] for h in range(part)], axis=1)
        weights = wo_vm[pl.ds(pl.multiple_of(first * HSIZE, HSIZE), part * HSIZE), :]
        return jnp.dot(attended, weights, preferred_element_type=jnp.float32)

    total_ref[...] = mix(first)
    mixed = total_ref[...] + mix(part - first)
    out_ref[...] = (mixed * gate_ref[pl.ds(my_video, 1), :]).astype(out_ref.dtype)

    def drain(i, _):
        h = lax.rem(i, HEADS)
        dest, copy = ship(h, i // HEADS)

        @pl.when(dest != me)
        def _():
            copy.wait_send()

        return 0

    lax.fori_loop(0, HEADS * teams, drain, 0)

    @pl.when(active)
    def _():
        def drain_forward(i, _):
            forward(i * 2 + core).wait_send()
            return 0

        lax.fori_loop(0, pairs, drain_forward, 0)

        def drain_back(t, _):
            s, copy = back(t)

            @pl.when(s != me)
            def _():
                copy.wait_send()

            return 0

        lax.fori_loop(0, mine, drain_back, 0)


def large(tokens, held_block, lengths, shift, scale, gate, w_qkv, w_out):
    count = lax.axis_size("seq")
    rows, width = tokens.shape
    pairs = count // 2
    teams = pairs // HEADS
    slots = -(-pairs // teams)
    vmem = pl.BlockSpec(memory_space=pltpu.VMEM)
    hbm = pl.BlockSpec(memory_space=pltpu.HBM)
    dma = pltpu.SemaphoreType.DMA
    return pl.pallas_call(
        functools.partial(kernel, count),
        out_shape=jax.ShapeDtypeStruct((rows, width), jnp.bfloat16),
        in_specs=[hbm] * 8,
        out_specs=vmem,
        scratch_shapes=[
            pltpu.SMEM(held_block.shape, jnp.int32),
            pltpu.SMEM(lengths.shape, jnp.int32),
            pltpu.VMEM(tokens.shape, tokens.dtype),
            pltpu.VMEM(shift.shape, jnp.float32),
            pltpu.VMEM(scale.shape, jnp.float32),
            pltpu.VMEM(gate.shape, jnp.float32),
            pltpu.VMEM((HEADS, width, 3 * HSIZE), jnp.bfloat16),
            pltpu.VMEM(w_out.shape, jnp.bfloat16),
            pltpu.VMEM((rows, width), jnp.bfloat16),
            pltpu.VMEM((HEADS, rows, 3 * HSIZE), jnp.bfloat16),
            pltpu.VMEM((count, rows, 3 * HSIZE), jnp.bfloat16),
            pltpu.VMEM((slots, rows, HSIZE), jnp.bfloat16),
            pltpu.VMEM((HEADS, rows, HSIZE), jnp.bfloat16),
            pltpu.VMEM((rows, width), jnp.float32),
            pltpu.SMEM((count,), jnp.int32),
            dma((6,)),
            dma((HEADS, 3)),
            dma,
            dma((HEADS, teams)),
            dma((count,)),
            dma((pairs,)),
            dma((slots,)),
            dma((HEADS,)),
        ],
        compiler_params=pltpu.CompilerParams(
            collective_id=0, has_side_effects=True, vmem_limit_bytes=61 * 1024 * 1024
        ),
    )(held_block, lengths, tokens, shift, scale, gate, w_qkv, w_out)


def shards(*args):
    return small(*args) if lax.axis_size("seq") == 16 else large(*args)


def solution(mesh):
    placed = (
        P(("groups", "seq"), None),
        P("groups"),
        P("groups"),
        P("groups", None),
        P("groups", None),
        P("groups", None),
        P(),
        P(),
    )
    return jax.shard_map(
        shards, mesh=mesh, in_specs=placed, out_specs=P(("groups", "seq"), None), check_vma=False
    )
```

```python
import functools
import math

import jax
import jax.numpy as jnp
from jax import lax
from jax.experimental import pallas as pl
from jax.experimental.pallas import tpu as pltpu
from jax.sharding import PartitionSpec as P

HEADS = 6
HSIZE = 128
MESH = pl.DeviceIdType.MESH
NEG = -math.inf
LIMIT = 24


def spread(
    count,
    held_hbm,
    len_hbm,
    tok_hbm,
    shift_hbm,
    scale_hbm,
    gate_hbm,
    w_hbm,
    att_out,
    gate_out,
    held_ref,
    len_ref,
    tok_ref,
    shift_ref,
    scale_ref,
    gate_ref,
    wkv_vm,
    wq_vm,
    norm_vm,
    tkv,
    tq,
    rkv,
    rq,
    ao,
    att,
    holder,
    in_sem,
    w_sem,
    wq_sem,
    tkv_sem,
    rkv_sem,
    tq_sem,
    rq_sem,
    fwd_sem,
    ao_sem,
    att_sem,
):
    rows, _ = tok_ref.shape
    nvid = len_ref.shape[0]
    pairs = count // 2
    me = lax.axis_index("seq")
    layers = count // 4
    z = me // 4
    y = lax.rem(me // 2, 2)
    core = lax.rem(me, 2)
    low_half = z < layers // 2
    chip = me // 2
    active = jnp.logical_and(chip >= 1, chip <= HEADS)
    my_head = jnp.where(active, chip - 1, 0)
    sibling = chip * 2 + 1 - core
    half = HEADS // 2

    barrier = pltpu.get_barrier_semaphore()

    def head_at(i):
        upper = lax.rem(i // half + jnp.where(low_half, 1, 0), 2)
        k = lax.rem(i, half)
        middle = upper * (half - 1) + 1 + lax.rem(k + y + core, half - 1)
        return jnp.where(k == 0, upper * (HEADS - 1), middle)

    def load_w(h, part):
        return pltpu.make_async_copy(
            w_hbm.at[:, pl.ds(pl.multiple_of(((part + 1) * HEADS + h) * HSIZE, HSIZE), HSIZE)],
            wkv_vm.at[h, :, pl.ds(part * HSIZE, HSIZE)],
            w_sem.at[h, part],
        )

    loads = [
        pltpu.make_async_copy(src, dst, in_sem.at[i])
        for i, (src, dst) in enumerate(
            (
                (tok_hbm, tok_ref),
                (held_hbm, held_ref),
                (len_hbm, len_ref),
                (shift_hbm, shift_ref),
                (scale_hbm, scale_ref),
                (gate_hbm, gate_ref),
            )
        )
    ]
    for load in loads:
        load.start()
    for part in range(2):
        load_w(head_at(0), part).start()

    def greet(i, _):
        d = lax.rem(me + i, count)
        pl.semaphore_signal(barrier, inc=1, device_id={"seq": d}, device_id_type=MESH)
        return 0

    lax.fori_loop(1, count, greet, 0, unroll=5)

    for i in range(1, HEADS):
        for part in range(2):
            load_w(head_at(i), part).start()
    load_q = pltpu.make_async_copy(w_hbm.at[:, 0 : HEADS * HSIZE], wq_vm, wq_sem)
    load_q.start()

    def span(block):
        video = jnp.int32(0)
        start = jnp.int32(0)
        end = len_ref[0]
        run = len_ref[0]
        for v in range(1, nvid):
            nxt = run + len_ref[v]
            inside = block >= run
            video = jnp.where(inside, v, video)
            start = jnp.where(inside, run, start)
            end = jnp.where(inside, nxt, end)
            run = nxt
        return video, start, end

    for load in loads:
        load.wait()
    my_video, _, _ = span(held_ref[me])

    x = tok_ref[...].astype(jnp.float32)
    mean = jnp.mean(x, axis=1, keepdims=True)
    x = x - mean
    var = jnp.mean(x * x, axis=1, keepdims=True)
    x = x * lax.rsqrt(var + 1e-6)
    x = x * (1.0 + scale_ref[pl.ds(my_video, 1), :]) + shift_ref[pl.ds(my_video, 1), :]
    norm_vm[...] = x.astype(jnp.bfloat16)

    def target(h):
        return (h + 1) * 2 + core

    def ship(h, src, dst, send, recv):
        return pltpu.make_async_remote_copy(
            src_ref=src.at[h],
            dst_ref=dst.at[me],
            send_sem=send.at[h],
            recv_sem=recv.at[me],
            device_id={"seq": target(h)},
            device_id_type=MESH,
        )

    def dispatch(h, src, dst, send, recv):
        dest = target(h)

        @pl.when(dest == me)
        def _():
            pltpu.make_async_copy(src.at[h], dst.at[me], recv.at[me]).start()

        @pl.when(dest != me)
        def _():
            ship(h, src, dst, send, recv).start()

    def project(i):
        h = head_at(i)
        for part in range(2):
            load_w(h, part).wait()
        tkv[h] = jnp.dot(norm_vm[...], wkv_vm[h], preferred_element_type=jnp.float32).astype(
            jnp.bfloat16
        )

    def send_kv(i, _):
        project(i)
        dispatch(head_at(i), tkv, rkv, tkv_sem, rkv_sem)
        return 0

    project(0)
    pl.semaphore_wait(barrier, count - 1)
    dispatch(head_at(0), tkv, rkv, tkv_sem, rkv_sem)
    lax.fori_loop(1, HEADS, send_kv, 0)

    load_q.wait()
    queries = jnp.dot(norm_vm[...], wq_vm[...], preferred_element_type=jnp.float32).astype(
        jnp.bfloat16
    )
    for h in range(HEADS):
        tq[h] = queries[:, h * HSIZE : (h + 1) * HSIZE]

    def send_q(i, _):
        dispatch(head_at(i), tq, rq, tq_sem, rq_sem)
        return 0

    lax.fori_loop(0, HEADS, send_q, 0)

    gate_out[...] = gate_ref[pl.ds(my_video, 1), :]

    def find(b, _):
        def look(d, acc):
            return jnp.where(held_ref[d] == b, d, acc)

        holder[b] = lax.fori_loop(0, count, look, jnp.int32(0), unroll=16)
        return 0

    lax.fori_loop(0, count, find, 0)

    def order(i):
        return jnp.where(low_half, pairs - 1 - i, i)

    def forward(t):
        s = t * 2 + core
        return pltpu.make_async_remote_copy(
            src_ref=rkv.at[s],
            dst_ref=rkv.at[s],
            send_sem=fwd_sem.at[t],
            recv_sem=rkv_sem.at[s],
            device_id={"seq": sibling},
            device_id_type=MESH,
        )

    chunk = count // 2
    inv = math.log2(math.e) / math.sqrt(HSIZE)

    def back(t):
        s = t * 2 + core
        return s, pltpu.make_async_remote_copy(
            src_ref=ao.at[t],
            dst_ref=att.at[my_head],
            send_sem=ao_sem.at[t],
            recv_sem=att_sem.at[my_head],
            device_id={"seq": s},
            device_id_type=MESH,
        )

    @pl.when(active)
    def _():
        def relay(i, _):
            t = order(lax.rem(i + pairs // 2, pairs))
            s = t * 2 + core
            pltpu.make_async_copy(rkv.at[s], rkv.at[s], rkv_sem.at[s]).wait()
            forward(t).start()
            return 0

        lax.fori_loop(0, pairs, relay, 0)

        def gather(i, _):
            s = order(lax.rem(i + pairs // 2, pairs)) * 2 + 1 - core
            pltpu.make_async_copy(rkv.at[s], rkv.at[s], rkv_sem.at[s]).wait()
            return 0

        lax.fori_loop(0, pairs, gather, 0)

        def attend(t):
            s = t * 2 + core
            _, start, end = span(held_ref[s])
            query = rq[s]
            slots = [
                holder[jnp.maximum(jnp.minimum(start + j, end - 1), 0)] for j in range(chunk)
            ]
            keys = jnp.concatenate([rkv[slot, :, 0:HSIZE] for slot in slots], axis=0)
            values = jnp.concatenate([rkv[slot, :, HSIZE : 2 * HSIZE] for slot in slots], axis=0)
            scores = lax.dot_general(
                query, keys, (((1,), (1,)), ((), ())), preferred_element_type=jnp.float32
            )
            scores = [scores[:, j * HSIZE : (j + 1) * HSIZE] for j in range(chunk)]
            top = jnp.max(functools.reduce(jnp.maximum, scores), axis=1, keepdims=True)
            weights = [
                jnp.exp2((scores[j] - jnp.where(start + j < end, top, math.inf)) * inv)
                for j in range(chunk)
            ]
            total = jnp.sum(functools.reduce(jnp.add, weights), axis=1, keepdims=True)
            weight16 = jnp.concatenate([weight.astype(jnp.bfloat16) for weight in weights], axis=1)
            summed = jnp.dot(weight16, values, preferred_element_type=jnp.float32)
            return (summed / total).astype(jnp.bfloat16)

        def answer(i, _):
            some = [order(i), jnp.where(low_half, 0, pairs // 2) + i]
            for t in some:
                s = t * 2 + core
                pltpu.make_async_copy(rq.at[s], rq.at[s], rq_sem.at[s]).wait()
            for t, value in zip(some, [attend(t) for t in some]):
                s, copy = back(t)
                ao[t] = value

                @pl.when(s == me)
                def _():
                    pltpu.make_async_copy(ao.at[t], att.at[my_head], att_sem.at[my_head]).start()

                @pl.when(s != me)
                def _():
                    copy.start()

            return 0

        lax.fori_loop(0, pairs // 2, answer, 0)

    for h in range(HEADS):
        pltpu.make_async_copy(att.at[h], att.at[h], att_sem.at[h]).wait()
        att_out[:, h * HSIZE : (h + 1) * HSIZE] = att[h]

    def drain(h, _):
        @pl.when(target(h) != me)
        def _():
            ship(h, tkv, rkv, tkv_sem, rkv_sem).wait_send()
            ship(h, tq, rq, tq_sem, rq_sem).wait_send()

        return 0

    lax.fori_loop(0, HEADS, drain, 0)

    @pl.when(active)
    def _():
        def drain_back(t, _):
            forward(t).wait_send()
            s, copy = back(t)

            @pl.when(s != me)
            def _():
                copy.wait_send()

            return 0

        lax.fori_loop(0, pairs, drain_back, 0)


def finish(att_ref, gate_ref, wo_ref, out_ref):
    mixed = jnp.dot(att_ref[...], wo_ref[...], preferred_element_type=jnp.float32)
    out_ref[...] = (mixed * gate_ref[...]).astype(out_ref.dtype)


def small(tokens, held_block, lengths, shift, scale, gate, w_qkv, w_out):
    count = lax.axis_size("seq")
    rows, width = tokens.shape
    pairs = count // 2
    wide = HEADS * HSIZE
    vmem = pl.BlockSpec(memory_space=pltpu.VMEM)
    hbm = pl.BlockSpec(memory_space=pltpu.HBM)
    dma = pltpu.SemaphoreType.DMA
    half = jnp.bfloat16
    pinned = [
        pltpu.with_memory_space_constraint(x, pltpu.HBM)
        for x in (held_block, lengths, tokens, shift, scale, gate, w_qkv)
    ]
    attended, row = pl.pallas_call(
        functools.partial(spread, count),
        out_shape=(
            jax.ShapeDtypeStruct((rows, wide), half),
            jax.ShapeDtypeStruct((1, width), jnp.float32),
        ),
        in_specs=[hbm] * 7,
        out_specs=(vmem, vmem),
        scratch_shapes=[
            pltpu.SMEM(held_block.shape, jnp.int32),
            pltpu.SMEM(lengths.shape, jnp.int32),
            pltpu.VMEM(tokens.shape, tokens.dtype),
            pltpu.VMEM(shift.shape, jnp.float32),
            pltpu.VMEM(scale.shape, jnp.float32),
            pltpu.VMEM(gate.shape, jnp.float32),
            pltpu.VMEM((HEADS, width, 2 * HSIZE), half),
            pltpu.VMEM((width, wide), half),
            pltpu.VMEM((rows, width), half),
            pltpu.VMEM((HEADS, rows, 2 * HSIZE), half),
            pltpu.VMEM((HEADS, rows, HSIZE), half),
            pltpu.VMEM((count, rows, 2 * HSIZE), half),
            pltpu.VMEM((count, rows, HSIZE), half),
            pltpu.VMEM((pairs, rows, HSIZE), half),
            pltpu.VMEM((HEADS, rows, HSIZE), half),
            pltpu.SMEM((count,), jnp.int32),
            dma((6,)),
            dma((HEADS, 2)),
            dma,
            dma((HEADS,)),
            dma((count,)),
            dma((HEADS,)),
            dma((count,)),
            dma((pairs,)),
            dma((pairs,)),
            dma((HEADS,)),
        ],
        compiler_params=pltpu.CompilerParams(
            collective_id=1, has_side_effects=True, vmem_limit_bytes=LIMIT * 1024 * 1024
        ),
    )(*pinned)
    return pl.pallas_call(
        finish,
        out_shape=jax.ShapeDtypeStruct((rows, width), half),
        in_specs=[vmem] * 3,
        out_specs=vmem,
        compiler_params=pltpu.CompilerParams(vmem_limit_bytes=LIMIT * 1024 * 1024),
    )(attended, row, w_out)


def kernel(
    count,
    held_hbm,
    len_hbm,
    tok_hbm,
    shift_hbm,
    scale_hbm,
    gate_hbm,
    w_hbm,
    wo_hbm,
    out_ref,
    held_ref,
    len_ref,
    tok_ref,
    shift_ref,
    scale_ref,
    gate_ref,
    w_vm,
    wo_vm,
    norm_vm,
    tx,
    rx,
    ao,
    att,
    total_ref,
    holder,
    in_sem,
    w_sem,
    wo_sem,
    tx_sem,
    rx_sem,
    fwd_sem,
    ao_sem,
    att_sem,
):
    rows, _ = tok_ref.shape
    nvid = len_ref.shape[0]
    pairs = count // 2
    teams = pairs // HEADS
    shift = (pairs - teams * HEADS) // 2
    me = lax.axis_index("seq")
    chip = me // 2
    core = lax.rem(me, 2)
    sibling = chip * 2 + 1 - core

    barrier = pltpu.get_barrier_semaphore()

    def greet(i, _):
        d = lax.rem(chip + i, pairs) * 2 + core
        pl.semaphore_signal(barrier, inc=1, device_id={"seq": d}, device_id_type=MESH)
        return 0

    lax.fori_loop(1, pairs, greet, 0, unroll=7)
    pl.semaphore_signal(barrier, inc=1, device_id={"seq": sibling}, device_id_type=MESH)

    low_half = chip < pairs // 2

    def head_at(i):
        first = jnp.where(low_half, HEADS // 2, 0) if teams == 1 else 0
        part = HEADS // 2
        return lax.rem(i // part * part + first, HEADS) + lax.rem(i + chip // 2 + chip, part)

    def load_w(h, part):
        return pltpu.make_async_copy(
            w_hbm.at[:, pl.ds(pl.multiple_of((part * HEADS + h) * HSIZE, HSIZE), HSIZE)],
            w_vm.at[h, :, pl.ds(part * HSIZE, HSIZE)],
            w_sem.at[h, part],
        )

    loads = [
        pltpu.make_async_copy(src, dst, in_sem.at[i])
        for i, (src, dst) in enumerate(
            (
                (tok_hbm, tok_ref),
                (held_hbm, held_ref),
                (len_hbm, len_ref),
                (shift_hbm, shift_ref),
                (scale_hbm, scale_ref),
                (gate_hbm, gate_ref),
            )
        )
    ]
    for load in loads:
        load.start()
    for i in range(HEADS // 2):
        for part in range(3):
            load_w(head_at(i), part).start()
    load_wo = pltpu.make_async_copy(wo_hbm, wo_vm, wo_sem)

    def span(block):
        video = jnp.int32(0)
        start = jnp.int32(0)
        end = len_ref[0]
        run = len_ref[0]
        for v in range(1, nvid):
            nxt = run + len_ref[v]
            inside = block >= run
            video = jnp.where(inside, v, video)
            start = jnp.where(inside, run, start)
            end = jnp.where(inside, nxt, end)
            run = nxt
        return video, start, end

    for load in loads:
        load.wait()
    my_video, _, _ = span(held_ref[me])

    x = tok_ref[...].astype(jnp.float32)
    mean = jnp.mean(x, axis=1, keepdims=True)
    x = x - mean
    var = jnp.mean(x * x, axis=1, keepdims=True)
    x = x * lax.rsqrt(var + 1e-6)
    x = x * (1.0 + scale_ref[pl.ds(my_video, 1), :]) + shift_ref[pl.ds(my_video, 1), :]
    norm_vm[...] = x.astype(jnp.bfloat16)

    for i in range(HEADS // 2, HEADS):
        for part in range(3):
            load_w(head_at(i), part).start()
    pl.semaphore_wait(barrier, pairs)

    def ship(h, team):
        dest = (team * HEADS + h + shift) * 2 + core
        return dest, pltpu.make_async_remote_copy(
            src_ref=tx.at[h],
            dst_ref=rx.at[me],
            send_sem=tx_sem.at[h, team],
            recv_sem=rx_sem.at[me],
            device_id={"seq": dest},
            device_id_type=MESH,
        )

    def project(i, _):
        h = head_at(i)
        for part in range(3):
            load_w(h, part).wait()
        tx[h] = jnp.dot(norm_vm[...], w_vm[h], preferred_element_type=jnp.float32).astype(
            jnp.bfloat16
        )

        def send(team, _):
            dest, copy = ship(h, team)

            @pl.when(dest == me)
            def _():
                pltpu.make_async_copy(tx.at[h], rx.at[me], rx_sem.at[me]).start()

            @pl.when(dest != me)
            def _():
                copy.start()

            return 0

        lax.fori_loop(0, teams, send, 0)
        return 0

    lax.fori_loop(0, HEADS, project, 0)

    load_wo.start()

    def find(b, _):
        def look(d, acc):
            return jnp.where(held_ref[d] == b, d, acc)

        holder[b] = lax.fori_loop(0, count, look, jnp.int32(0), unroll=16)
        return 0

    lax.fori_loop(0, count, find, 0)

    active = jnp.logical_and(chip >= shift, chip < teams * HEADS + shift)
    place = jnp.where(active, chip - shift, 0)
    my_head = lax.rem(place, HEADS)
    my_team = place // HEADS
    near = jnp.where(low_half, 0, pairs // 2)
    kv_cols = pl.ds(HSIZE, 2 * HSIZE)

    def forward(s):
        return pltpu.make_async_remote_copy(
            src_ref=rx.at[s, :, kv_cols],
            dst_ref=rx.at[s, :, kv_cols],
            send_sem=fwd_sem.at[s // 2],
            recv_sem=rx_sem.at[s],
            device_id={"seq": sibling},
            device_id_type=MESH,
        )

    key_blocks = count // 2
    chunk = min(8, key_blocks)
    turns = key_blocks // chunk
    mine = pairs if teams == 1 else (pairs - my_team + teams - 1) // teams
    width = 2 if teams == 1 and pairs % 2 == 0 else 1
    inv = math.log2(math.e) / math.sqrt(HSIZE)

    def back(t):
        s = (my_team + t * teams) * 2 + core
        return s, pltpu.make_async_remote_copy(
            src_ref=ao.at[t],
            dst_ref=att.at[my_head],
            send_sem=ao_sem.at[t],
            recv_sem=att_sem.at[my_head],
            device_id={"seq": s},
            device_id_type=MESH,
        )

    @pl.when(active)
    def _():
        def relay(i, _):
            s = lax.rem(i + near, pairs) * 2 + core
            pltpu.make_async_copy(rx.at[s], rx.at[s], rx_sem.at[s]).wait()
            forward(s).start()
            return 0

        lax.fori_loop(0, pairs, relay, 0)

        def gather(i, _):
            s = lax.rem(i + near, pairs) * 2 + 1 - core
            part = rx.at[s, :, kv_cols]
            pltpu.make_async_copy(part, part, rx_sem.at[s]).wait()
            return 0

        lax.fori_loop(0, pairs, gather, 0)

        def attend(t):
            s, _ = back(t)
            _, start, end = span(held_ref[s])
            query = rx[s, :, 0:HSIZE]

            def key_turn(turn, carry):
                top, total, summed = carry
                scores = []
                where = []
                for j in range(chunk):
                    block = start + turn * chunk + j
                    slot = holder[jnp.maximum(jnp.minimum(block, end - 1), 0)]
                    where.append(slot)
                    score = lax.dot_general(
                        query,
                        rx[slot, :, HSIZE : 2 * HSIZE],
                        (((1,), (1,)), ((), ())),
                        preferred_element_type=jnp.float32,
                    )
                    bias = jnp.where(block < end, 0.0, NEG)
                    scores.append(score + bias)
                high = functools.reduce(jnp.maximum, scores)
                new_top = jnp.maximum(top, jnp.max(high, axis=1, keepdims=True))
                factor = jnp.exp2((top - new_top) * inv)
                total = total * factor
                summed = summed * factor
                sums = None
                for j in range(chunk):
                    weight = jnp.exp2((scores[j] - new_top) * inv)
                    sums = weight if sums is None else sums + weight
                    summed = summed + jnp.dot(
                        weight.astype(jnp.bfloat16),
                        rx[where[j], :, 2 * HSIZE : 3 * HSIZE],
                        preferred_element_type=jnp.float32,
                    )
                total = total + jnp.sum(sums, axis=1, keepdims=True)
                return new_top, total, summed

            carry = (
                jnp.full((rows, 1), NEG, jnp.float32),
                jnp.zeros((rows, 1), jnp.float32),
                jnp.zeros((rows, HSIZE), jnp.float32),
            )
            if turns == 1:
                carry = key_turn(0, carry)
            else:
                carry = lax.fori_loop(0, turns, key_turn, carry)
            _, total, summed = carry
            return (summed / total).astype(jnp.bfloat16)

        def answer(i, _):
            some = [
                lax.rem(i * width + u + jnp.where(low_half, mine // 2, 0), mine)
                for u in range(width)
            ]
            for t, value in zip(some, [attend(t) for t in some]):
                s, copy = back(t)
                ao[t] = value

                @pl.when(s == me)
                def _():
                    pltpu.make_async_copy(ao.at[t], att.at[my_head], att_sem.at[my_head]).start()

                @pl.when(s != me)
                def _():
                    copy.start()

            return 0

        lax.fori_loop(0, mine // width, answer, 0)

    load_wo.wait()
    part = HEADS // 2
    first = jnp.where(low_half, 0, part) if teams == 1 else 0

    def mix(first):
        for h in range(part):
            pltpu.make_async_copy(att.at[first + h], att.at[first + h], att_sem.at[first + h]).wait()
        attended = jnp.concatenate([att[first + h] for h in range(part)], axis=1)
        weights = wo_vm[pl.ds(pl.multiple_of(first * HSIZE, HSIZE), part * HSIZE), :]
        return jnp.dot(attended, weights, preferred_element_type=jnp.float32)

    total_ref[...] = mix(first)
    mixed = total_ref[...] + mix(part - first)
    out_ref[...] = (mixed * gate_ref[pl.ds(my_video, 1), :]).astype(out_ref.dtype)

    def drain(i, _):
        h = lax.rem(i, HEADS)
        dest, copy = ship(h, i // HEADS)

        @pl.when(dest != me)
        def _():
            copy.wait_send()

        return 0

    lax.fori_loop(0, HEADS * teams, drain, 0)

    @pl.when(active)
    def _():
        def drain_forward(i, _):
            forward(i * 2 + core).wait_send()
            return 0

        lax.fori_loop(0, pairs, drain_forward, 0)

        def drain_back(t, _):
            s, copy = back(t)

            @pl.when(s != me)
            def _():
                copy.wait_send()

            return 0

        lax.fori_loop(0, mine, drain_back, 0)


def large(tokens, held_block, lengths, shift, scale, gate, w_qkv, w_out):
    count = lax.axis_size("seq")
    rows, width = tokens.shape
    pairs = count // 2
    teams = pairs // HEADS
    slots = -(-pairs // teams)
    vmem = pl.BlockSpec(memory_space=pltpu.VMEM)
    hbm = pl.BlockSpec(memory_space=pltpu.HBM)
    dma = pltpu.SemaphoreType.DMA
    return pl.pallas_call(
        functools.partial(kernel, count),
        out_shape=jax.ShapeDtypeStruct((rows, width), jnp.bfloat16),
        in_specs=[hbm] * 8,
        out_specs=vmem,
        scratch_shapes=[
            pltpu.SMEM(held_block.shape, jnp.int32),
            pltpu.SMEM(lengths.shape, jnp.int32),
            pltpu.VMEM(tokens.shape, tokens.dtype),
            pltpu.VMEM(shift.shape, jnp.float32),
            pltpu.VMEM(scale.shape, jnp.float32),
            pltpu.VMEM(gate.shape, jnp.float32),
            pltpu.VMEM((HEADS, width, 3 * HSIZE), jnp.bfloat16),
            pltpu.VMEM(w_out.shape, jnp.bfloat16),
            pltpu.VMEM((rows, width), jnp.bfloat16),
            pltpu.VMEM((HEADS, rows, 3 * HSIZE), jnp.bfloat16),
            pltpu.VMEM((count, rows, 3 * HSIZE), jnp.bfloat16),
            pltpu.VMEM((slots, rows, HSIZE), jnp.bfloat16),
            pltpu.VMEM((HEADS, rows, HSIZE), jnp.bfloat16),
            pltpu.VMEM((rows, width), jnp.float32),
            pltpu.SMEM((count,), jnp.int32),
            dma((6,)),
            dma((HEADS, 3)),
            dma,
            dma((HEADS, teams)),
            dma((count,)),
            dma((pairs,)),
            dma((slots,)),
            dma((HEADS,)),
        ],
        compiler_params=pltpu.CompilerParams(
            collective_id=0, has_side_effects=True, vmem_limit_bytes=61 * 1024 * 1024
        ),
    )(held_block, lengths, tokens, shift, scale, gate, w_qkv, w_out)


def shards(*args):
    return small(*args) if lax.axis_size("seq") == 16 else large(*args)


def solution(mesh):
    placed = (
        P(("groups", "seq"), None),
        P("groups"),
        P("groups"),
        P("groups", None),
        P("groups", None),
        P("groups", None),
        P(),
        P(),
    )
    return jax.shard_map(
        shards, mesh=mesh, in_specs=placed, out_specs=P(("groups", "seq"), None), check_vma=False
    )
```

```python
import functools
import math

import jax
import jax.numpy as jnp
from jax import lax
from jax.experimental import pallas as pl
from jax.experimental.pallas import tpu as pltpu
from jax.sharding import PartitionSpec as P

HEADS = 6
HSIZE = 128
MESH = pl.DeviceIdType.MESH
NEG = -math.inf
LIMIT = 24


def spread(
    count,
    held_hbm,
    len_hbm,
    tok_hbm,
    shift_hbm,
    scale_hbm,
    gate_hbm,
    w_hbm,
    wo_hbm,
    att_out,
    gate_out,
    part_out,
    held_ref,
    len_ref,
    tok_ref,
    shift_ref,
    scale_ref,
    gate_ref,
    wkv_vm,
    wq_vm,
    wo_vm,
    norm_vm,
    tkv,
    tq,
    rkv,
    rq,
    ao,
    att,
    holder,
    in_sem,
    w_sem,
    wq_sem,
    wo_sem,
    tkv_sem,
    rkv_sem,
    tq_sem,
    rq_sem,
    fwd_sem,
    ao_sem,
    att_sem,
):
    rows, _ = tok_ref.shape
    nvid = len_ref.shape[0]
    pairs = count // 2
    me = lax.axis_index("seq")
    layers = count // 4
    z = me // 4
    y = lax.rem(me // 2, 2)
    core = lax.rem(me, 2)
    low_half = z < layers // 2
    chip = me // 2
    active = jnp.logical_and(chip >= 1, chip <= HEADS)
    my_head = jnp.where(active, chip - 1, 0)
    sibling = chip * 2 + 1 - core
    half = HEADS // 2

    barrier = pltpu.get_barrier_semaphore()

    def head_at(i):
        upper = lax.rem(i // half + jnp.where(low_half, 1, 0), 2)
        k = lax.rem(i, half)
        middle = upper * (half - 1) + 1 + lax.rem(k + y + 1 - core, half - 1)
        return jnp.where(k == 0, upper * (HEADS - 1), middle)

    def load_w(h, part):
        return pltpu.make_async_copy(
            w_hbm.at[:, pl.ds(pl.multiple_of(((part + 1) * HEADS + h) * HSIZE, HSIZE), HSIZE)],
            wkv_vm.at[h, :, pl.ds(part * HSIZE, HSIZE)],
            w_sem.at[h, part],
        )

    loads = [
        pltpu.make_async_copy(src, dst, in_sem.at[i])
        for i, (src, dst) in enumerate(
            (
                (tok_hbm, tok_ref),
                (held_hbm, held_ref),
                (len_hbm, len_ref),
                (shift_hbm, shift_ref),
                (scale_hbm, scale_ref),
                (gate_hbm, gate_ref),
            )
        )
    ]
    for load in loads:
        load.start()
    for part in range(2):
        load_w(head_at(0), part).start()

    def greet(i, _):
        d = lax.rem(me + i, count)
        pl.semaphore_signal(barrier, inc=1, device_id={"seq": d}, device_id_type=MESH)
        return 0

    lax.fori_loop(1, count, greet, 0, unroll=5)

    for i in range(1, HEADS):
        for part in range(2):
            load_w(head_at(i), part).start()
    load_q = pltpu.make_async_copy(w_hbm.at[:, 0 : HEADS * HSIZE], wq_vm, wq_sem)
    load_q.start()
    own = jnp.where(low_half, 0, half)
    load_wo = pltpu.make_async_copy(
        wo_hbm.at[pl.ds(pl.multiple_of(own * HSIZE, HSIZE), half * HSIZE), :], wo_vm, wo_sem
    )
    load_wo.start()

    def span(block):
        video = jnp.int32(0)
        start = jnp.int32(0)
        end = len_ref[0]
        run = len_ref[0]
        for v in range(1, nvid):
            nxt = run + len_ref[v]
            inside = block >= run
            video = jnp.where(inside, v, video)
            start = jnp.where(inside, run, start)
            end = jnp.where(inside, nxt, end)
            run = nxt
        return video, start, end

    loads[0].wait()
    x = tok_ref[...].astype(jnp.float32)
    mean = jnp.mean(x, axis=1, keepdims=True)
    x = x - mean
    var = jnp.mean(x * x, axis=1, keepdims=True)
    x = x * lax.rsqrt(var + 1e-6)
    for load in loads[1:]:
        load.wait()
    my_video, _, _ = span(held_ref[me])
    x = x * (1.0 + scale_ref[pl.ds(my_video, 1), :]) + shift_ref[pl.ds(my_video, 1), :]
    norm_vm[...] = x.astype(jnp.bfloat16)

    def target(h):
        return (h + 1) * 2 + core

    def ship(h, src, dst, send, recv):
        return pltpu.make_async_remote_copy(
            src_ref=src.at[h],
            dst_ref=dst.at[me],
            send_sem=send.at[h],
            recv_sem=recv.at[me],
            device_id={"seq": target(h)},
            device_id_type=MESH,
        )

    def dispatch(h, src, dst, send, recv):
        dest = target(h)

        @pl.when(dest == me)
        def _():
            pltpu.make_async_copy(src.at[h], dst.at[me], recv.at[me]).start()

        @pl.when(dest != me)
        def _():
            ship(h, src, dst, send, recv).start()

    def project(i):
        h = head_at(i)
        for part in range(2):
            load_w(h, part).wait()
        tkv[h] = jnp.dot(norm_vm[...], wkv_vm[h], preferred_element_type=jnp.float32).astype(
            jnp.bfloat16
        )

    def send_kv(i, _):
        project(i)
        dispatch(head_at(i), tkv, rkv, tkv_sem, rkv_sem)
        return 0

    project(0)
    pl.semaphore_wait(barrier, count - 1)
    dispatch(head_at(0), tkv, rkv, tkv_sem, rkv_sem)
    lax.fori_loop(1, HEADS, send_kv, 0)

    load_q.wait()
    queries = jnp.dot(norm_vm[...], wq_vm[...], preferred_element_type=jnp.float32).astype(
        jnp.bfloat16
    )
    for h in range(HEADS):
        tq[h] = queries[:, h * HSIZE : (h + 1) * HSIZE]

    def send_q(i, _):
        dispatch(head_at(i), tq, rq, tq_sem, rq_sem)
        return 0

    lax.fori_loop(0, HEADS, send_q, 0)

    gate_out[...] = gate_ref[pl.ds(my_video, 1), :]

    def find(b, _):
        def look(d, acc):
            return jnp.where(held_ref[d] == b, d, acc)

        holder[b] = lax.fori_loop(0, count, look, jnp.int32(0), unroll=16)
        return 0

    lax.fori_loop(0, count, find, 0)

    def order(i):
        return jnp.where(low_half, pairs - 1 - i, i)

    def forward(t):
        s = t * 2 + core
        return pltpu.make_async_remote_copy(
            src_ref=rkv.at[s],
            dst_ref=rkv.at[s],
            send_sem=fwd_sem.at[t],
            recv_sem=rkv_sem.at[s],
            device_id={"seq": sibling},
            device_id_type=MESH,
        )

    chunk = count // 2
    inv = math.log2(math.e) / math.sqrt(HSIZE)

    def back(t):
        s = t * 2 + core
        return s, pltpu.make_async_remote_copy(
            src_ref=ao.at[t],
            dst_ref=att.at[my_head],
            send_sem=ao_sem.at[t],
            recv_sem=att_sem.at[my_head],
            device_id={"seq": s},
            device_id_type=MESH,
        )

    @pl.when(active)
    def _():
        def relay(i, _):
            t = order(lax.rem(i + pairs // 2, pairs))
            s = t * 2 + core
            pltpu.make_async_copy(rkv.at[s], rkv.at[s], rkv_sem.at[s]).wait()
            forward(t).start()
            return 0

        lax.fori_loop(0, pairs, relay, 0)

        def gather(i, _):
            s = order(lax.rem(i + pairs // 2, pairs)) * 2 + 1 - core
            pltpu.make_async_copy(rkv.at[s], rkv.at[s], rkv_sem.at[s]).wait()
            return 0

        lax.fori_loop(0, pairs, gather, 0)

        def attend(some):
            spans = []
            slots = []
            scores = []
            for t in some:
                s = t * 2 + core
                _, start, end = span(held_ref[s])
                slot = [
                    holder[jnp.maximum(jnp.minimum(start + j, end - 1), 0)] for j in range(chunk)
                ]
                keys = jnp.concatenate([rkv[d, :, 0:HSIZE] for d in slot], axis=0)
                score = lax.dot_general(
                    rq[s], keys, (((1,), (1,)), ((), ())), preferred_element_type=jnp.float32
                )
                spans.append((start, end))
                slots.append(slot)
                scores.append([score[:, j * HSIZE : (j + 1) * HSIZE] for j in range(chunk)])
            tops = [
                jnp.max(functools.reduce(jnp.maximum, score), axis=1, keepdims=True)
                for score in scores
            ]
            weights = [
                [
                    jnp.exp2((score[j] - jnp.where(start + j < end, top, math.inf)) * inv)
                    for j in range(chunk)
                ]
                for score, top, (start, end) in zip(scores, tops, spans)
            ]
            out = []
            for weight, slot in zip(weights, slots):
                values = jnp.concatenate(
                    [rkv[d, :, HSIZE : 2 * HSIZE] for d in slot], axis=0
                )
                weight16 = jnp.concatenate([w.astype(jnp.bfloat16) for w in weight], axis=1)
                summed = jnp.dot(weight16, values, preferred_element_type=jnp.float32)
                total = jnp.sum(functools.reduce(jnp.add, weight), axis=1, keepdims=True)
                out.append((summed / total).astype(jnp.bfloat16))
            return out

        def answer(i, _):
            some = [order(i), jnp.where(low_half, 0, pairs // 2) + i]
            for t in some:
                s = t * 2 + core
                pltpu.make_async_copy(rq.at[s], rq.at[s], rq_sem.at[s]).wait()
            for t, value in zip(some, attend(some)):
                s, copy = back(t)
                ao[t] = value

                @pl.when(s == me)
                def _():
                    pltpu.make_async_copy(ao.at[t], att.at[my_head], att_sem.at[my_head]).start()

                @pl.when(s != me)
                def _():
                    copy.start()

            return 0

        lax.fori_loop(0, pairs // 2, answer, 0)

    def arrived(first):
        for h in range(half):
            part = att.at[first + h]
            pltpu.make_async_copy(part, part, att_sem.at[first + h]).wait()
        return jnp.concatenate([att[first + h] for h in range(half)], axis=1)

    load_wo.wait()
    part_out[...] = jnp.dot(arrived(own), wo_vm[...], preferred_element_type=jnp.float32)
    att_out[...] = arrived(half - own)

    def drain(h, _):
        @pl.when(target(h) != me)
        def _():
            ship(h, tkv, rkv, tkv_sem, rkv_sem).wait_send()
            ship(h, tq, rq, tq_sem, rq_sem).wait_send()

        return 0

    lax.fori_loop(0, HEADS, drain, 0)

    @pl.when(active)
    def _():
        def drain_back(t, _):
            forward(t).wait_send()
            s, copy = back(t)

            @pl.when(s != me)
            def _():
                copy.wait_send()

            return 0

        lax.fori_loop(0, pairs, drain_back, 0)


def finish(count, att_ref, gate_ref, part_ref, wo_ref, out_ref):
    deep = att_ref.shape[1]
    first = jnp.where(lax.axis_index("seq") < count // 2, deep, 0)
    weights = wo_ref[pl.ds(pl.multiple_of(first, deep), deep), :]
    mixed = jnp.dot(att_ref[...], weights, preferred_element_type=jnp.float32)
    out_ref[...] = ((part_ref[...] + mixed) * gate_ref[...]).astype(out_ref.dtype)


def small(tokens, held_block, lengths, shift, scale, gate, w_qkv, w_out):
    count = lax.axis_size("seq")
    rows, width = tokens.shape
    pairs = count // 2
    wide = HEADS * HSIZE
    vmem = pl.BlockSpec(memory_space=pltpu.VMEM)
    hbm = pl.BlockSpec(memory_space=pltpu.HBM)
    dma = pltpu.SemaphoreType.DMA
    half = jnp.bfloat16
    pinned = [
        pltpu.with_memory_space_constraint(x, pltpu.HBM)
        for x in (held_block, lengths, tokens, shift, scale, gate, w_qkv, w_out)
    ]
    attended, row, part = pl.pallas_call(
        functools.partial(spread, count),
        out_shape=(
            jax.ShapeDtypeStruct((rows, wide // 2), half),
            jax.ShapeDtypeStruct((1, width), jnp.float32),
            jax.ShapeDtypeStruct((rows, width), jnp.float32),
        ),
        in_specs=[hbm] * 8,
        out_specs=(vmem, vmem, vmem),
        scratch_shapes=[
            pltpu.SMEM(held_block.shape, jnp.int32),
            pltpu.SMEM(lengths.shape, jnp.int32),
            pltpu.VMEM(tokens.shape, tokens.dtype),
            pltpu.VMEM(shift.shape, jnp.float32),
            pltpu.VMEM(scale.shape, jnp.float32),
            pltpu.VMEM(gate.shape, jnp.float32),
            pltpu.VMEM((HEADS, width, 2 * HSIZE), half),
            pltpu.VMEM((width, wide), half),
            pltpu.VMEM((wide // 2, width), half),
            pltpu.VMEM((rows, width), half),
            pltpu.VMEM((HEADS, rows, 2 * HSIZE), half),
            pltpu.VMEM((HEADS, rows, HSIZE), half),
            pltpu.VMEM((count, rows, 2 * HSIZE), half),
            pltpu.VMEM((count, rows, HSIZE), half),
            pltpu.VMEM((pairs, rows, HSIZE), half),
            pltpu.VMEM((HEADS, rows, HSIZE), half),
            pltpu.SMEM((count,), jnp.int32),
            dma((6,)),
            dma((HEADS, 2)),
            dma,
            dma,
            dma((HEADS,)),
            dma((count,)),
            dma((HEADS,)),
            dma((count,)),
            dma((pairs,)),
            dma((pairs,)),
            dma((HEADS,)),
        ],
        compiler_params=pltpu.CompilerParams(
            collective_id=1, has_side_effects=True, vmem_limit_bytes=LIMIT * 1024 * 1024
        ),
    )(*pinned)
    return pl.pallas_call(
        functools.partial(finish, count),
        out_shape=jax.ShapeDtypeStruct((rows, width), half),
        in_specs=[vmem] * 4,
        out_specs=vmem,
        compiler_params=pltpu.CompilerParams(vmem_limit_bytes=LIMIT * 1024 * 1024),
    )(attended, row, part, w_out)


def kernel(
    count,
    held_hbm,
    len_hbm,
    tok_hbm,
    shift_hbm,
    scale_hbm,
    gate_hbm,
    w_hbm,
    wo_hbm,
    out_ref,
    held_ref,
    len_ref,
    tok_ref,
    shift_ref,
    scale_ref,
    gate_ref,
    w_vm,
    wo_vm,
    norm_vm,
    tx,
    rx,
    ao,
    att,
    total_ref,
    holder,
    in_sem,
    w_sem,
    wo_sem,
    tx_sem,
    rx_sem,
    fwd_sem,
    ao_sem,
    att_sem,
):
    rows, _ = tok_ref.shape
    nvid = len_ref.shape[0]
    pairs = count // 2
    teams = pairs // HEADS
    shift = (pairs - teams * HEADS) // 2
    me = lax.axis_index("seq")
    chip = me // 2
    core = lax.rem(me, 2)
    sibling = chip * 2 + 1 - core

    barrier = pltpu.get_barrier_semaphore()

    def greet(i, _):
        d = lax.rem(chip + i, pairs) * 2 + core
        pl.semaphore_signal(barrier, inc=1, device_id={"seq": d}, device_id_type=MESH)
        return 0

    lax.fori_loop(1, pairs, greet, 0, unroll=7)
    pl.semaphore_signal(barrier, inc=1, device_id={"seq": sibling}, device_id_type=MESH)

    low_half = chip < pairs // 2

    def head_at(i):
        first = jnp.where(low_half, HEADS // 2, 0) if teams == 1 else 0
        part = HEADS // 2
        return lax.rem(i // part * part + first, HEADS) + lax.rem(i + chip // 2 + chip, part)

    def load_w(h, part):
        return pltpu.make_async_copy(
            w_hbm.at[:, pl.ds(pl.multiple_of((part * HEADS + h) * HSIZE, HSIZE), HSIZE)],
            w_vm.at[h, :, pl.ds(part * HSIZE, HSIZE)],
            w_sem.at[h, part],
        )

    loads = [
        pltpu.make_async_copy(src, dst, in_sem.at[i])
        for i, (src, dst) in enumerate(
            (
                (tok_hbm, tok_ref),
                (held_hbm, held_ref),
                (len_hbm, len_ref),
                (shift_hbm, shift_ref),
                (scale_hbm, scale_ref),
                (gate_hbm, gate_ref),
            )
        )
    ]
    for load in loads:
        load.start()
    for i in range(HEADS // 2):
        for part in range(3):
            load_w(head_at(i), part).start()
    load_wo = pltpu.make_async_copy(wo_hbm, wo_vm, wo_sem)

    def span(block):
        video = jnp.int32(0)
        start = jnp.int32(0)
        end = len_ref[0]
        run = len_ref[0]
        for v in range(1, nvid):
            nxt = run + len_ref[v]
            inside = block >= run
            video = jnp.where(inside, v, video)
            start = jnp.where(inside, run, start)
            end = jnp.where(inside, nxt, end)
            run = nxt
        return video, start, end

    for load in loads:
        load.wait()
    my_video, _, _ = span(held_ref[me])

    x = tok_ref[...].astype(jnp.float32)
    mean = jnp.mean(x, axis=1, keepdims=True)
    x = x - mean
    var = jnp.mean(x * x, axis=1, keepdims=True)
    x = x * lax.rsqrt(var + 1e-6)
    x = x * (1.0 + scale_ref[pl.ds(my_video, 1), :]) + shift_ref[pl.ds(my_video, 1), :]
    norm_vm[...] = x.astype(jnp.bfloat16)

    for i in range(HEADS // 2, HEADS):
        for part in range(3):
            load_w(head_at(i), part).start()
    pl.semaphore_wait(barrier, pairs)

    def ship(h, team):
        dest = (team * HEADS + h + shift) * 2 + core
        return dest, pltpu.make_async_remote_copy(
            src_ref=tx.at[h],
            dst_ref=rx.at[me],
            send_sem=tx_sem.at[h, team],
            recv_sem=rx_sem.at[me],
            device_id={"seq": dest},
            device_id_type=MESH,
        )

    def project(i, _):
        h = head_at(i)
        for part in range(3):
            load_w(h, part).wait()
        tx[h] = jnp.dot(norm_vm[...], w_vm[h], preferred_element_type=jnp.float32).astype(
            jnp.bfloat16
        )

        def send(team, _):
            dest, copy = ship(h, team)

            @pl.when(dest == me)
            def _():
                pltpu.make_async_copy(tx.at[h], rx.at[me], rx_sem.at[me]).start()

            @pl.when(dest != me)
            def _():
                copy.start()

            return 0

        lax.fori_loop(0, teams, send, 0)
        return 0

    lax.fori_loop(0, HEADS, project, 0)

    load_wo.start()

    def find(b, _):
        def look(d, acc):
            return jnp.where(held_ref[d] == b, d, acc)

        holder[b] = lax.fori_loop(0, count, look, jnp.int32(0), unroll=16)
        return 0

    lax.fori_loop(0, count, find, 0)

    active = jnp.logical_and(chip >= shift, chip < teams * HEADS + shift)
    place = jnp.where(active, chip - shift, 0)
    my_head = lax.rem(place, HEADS)
    my_team = place // HEADS
    near = jnp.where(low_half, 0, pairs // 2)
    kv_cols = pl.ds(HSIZE, 2 * HSIZE)

    def forward(s):
        return pltpu.make_async_remote_copy(
            src_ref=rx.at[s, :, kv_cols],
            dst_ref=rx.at[s, :, kv_cols],
            send_sem=fwd_sem.at[s // 2],
            recv_sem=rx_sem.at[s],
            device_id={"seq": sibling},
            device_id_type=MESH,
        )

    key_blocks = count // 2
    chunk = min(8, key_blocks)
    turns = key_blocks // chunk
    mine = pairs if teams == 1 else (pairs - my_team + teams - 1) // teams
    width = 2 if teams == 1 and pairs % 2 == 0 else 1
    inv = math.log2(math.e) / math.sqrt(HSIZE)

    def back(t):
        s = (my_team + t * teams) * 2 + core
        return s, pltpu.make_async_remote_copy(
            src_ref=ao.at[t],
            dst_ref=att.at[my_head],
            send_sem=ao_sem.at[t],
            recv_sem=att_sem.at[my_head],
            device_id={"seq": s},
            device_id_type=MESH,
        )

    @pl.when(active)
    def _():
        def relay(i, _):
            s = lax.rem(i + near, pairs) * 2 + core
            pltpu.make_async_copy(rx.at[s], rx.at[s], rx_sem.at[s]).wait()
            forward(s).start()
            return 0

        lax.fori_loop(0, pairs, relay, 0)

        def gather(i, _):
            s = lax.rem(i + near, pairs) * 2 + 1 - core
            part = rx.at[s, :, kv_cols]
            pltpu.make_async_copy(part, part, rx_sem.at[s]).wait()
            return 0

        lax.fori_loop(0, pairs, gather, 0)

        def attend(t):
            s, _ = back(t)
            _, start, end = span(held_ref[s])
            query = rx[s, :, 0:HSIZE]

            def key_turn(turn, carry):
                top, total, summed = carry
                scores = []
                where = []
                for j in range(chunk):
                    block = start + turn * chunk + j
                    slot = holder[jnp.maximum(jnp.minimum(block, end - 1), 0)]
                    where.append(slot)
                    score = lax.dot_general(
                        query,
                        rx[slot, :, HSIZE : 2 * HSIZE],
                        (((1,), (1,)), ((), ())),
                        preferred_element_type=jnp.float32,
                    )
                    bias = jnp.where(block < end, 0.0, NEG)
                    scores.append(score + bias)
                high = functools.reduce(jnp.maximum, scores)
                new_top = jnp.maximum(top, jnp.max(high, axis=1, keepdims=True))
                factor = jnp.exp2((top - new_top) * inv)
                total = total * factor
                summed = summed * factor
                sums = None
                for j in range(chunk):
                    weight = jnp.exp2((scores[j] - new_top) * inv)
                    sums = weight if sums is None else sums + weight
                    summed = summed + jnp.dot(
                        weight.astype(jnp.bfloat16),
                        rx[where[j], :, 2 * HSIZE : 3 * HSIZE],
                        preferred_element_type=jnp.float32,
                    )
                total = total + jnp.sum(sums, axis=1, keepdims=True)
                return new_top, total, summed

            carry = (
                jnp.full((rows, 1), NEG, jnp.float32),
                jnp.zeros((rows, 1), jnp.float32),
                jnp.zeros((rows, HSIZE), jnp.float32),
            )
            if turns == 1:
                carry = key_turn(0, carry)
            else:
                carry = lax.fori_loop(0, turns, key_turn, carry)
            _, total, summed = carry
            return (summed / total).astype(jnp.bfloat16)

        def answer(i, _):
            some = [
                lax.rem(i * width + u + jnp.where(low_half, mine // 2, 0), mine)
                for u in range(width)
            ]
            for t, value in zip(some, [attend(t) for t in some]):
                s, copy = back(t)
                ao[t] = value

                @pl.when(s == me)
                def _():
                    pltpu.make_async_copy(ao.at[t], att.at[my_head], att_sem.at[my_head]).start()

                @pl.when(s != me)
                def _():
                    copy.start()

            return 0

        lax.fori_loop(0, mine // width, answer, 0)

    load_wo.wait()
    part = HEADS // 2
    first = jnp.where(low_half, 0, part) if teams == 1 else 0

    def mix(first):
        for h in range(part):
            pltpu.make_async_copy(att.at[first + h], att.at[first + h], att_sem.at[first + h]).wait()
        attended = jnp.concatenate([att[first + h] for h in range(part)], axis=1)
        weights = wo_vm[pl.ds(pl.multiple_of(first * HSIZE, HSIZE), part * HSIZE), :]
        return jnp.dot(attended, weights, preferred_element_type=jnp.float32)

    total_ref[...] = mix(first)
    mixed = total_ref[...] + mix(part - first)
    out_ref[...] = (mixed * gate_ref[pl.ds(my_video, 1), :]).astype(out_ref.dtype)

    def drain(i, _):
        h = lax.rem(i, HEADS)
        dest, copy = ship(h, i // HEADS)

        @pl.when(dest != me)
        def _():
            copy.wait_send()

        return 0

    lax.fori_loop(0, HEADS * teams, drain, 0)

    @pl.when(active)
    def _():
        def drain_forward(i, _):
            forward(i * 2 + core).wait_send()
            return 0

        lax.fori_loop(0, pairs, drain_forward, 0)

        def drain_back(t, _):
            s, copy = back(t)

            @pl.when(s != me)
            def _():
                copy.wait_send()

            return 0

        lax.fori_loop(0, mine, drain_back, 0)


def large(tokens, held_block, lengths, shift, scale, gate, w_qkv, w_out):
    count = lax.axis_size("seq")
    rows, width = tokens.shape
    pairs = count // 2
    teams = pairs // HEADS
    slots = -(-pairs // teams)
    vmem = pl.BlockSpec(memory_space=pltpu.VMEM)
    hbm = pl.BlockSpec(memory_space=pltpu.HBM)
    dma = pltpu.SemaphoreType.DMA
    return pl.pallas_call(
        functools.partial(kernel, count),
        out_shape=jax.ShapeDtypeStruct((rows, width), jnp.bfloat16),
        in_specs=[hbm] * 8,
        out_specs=vmem,
        scratch_shapes=[
            pltpu.SMEM(held_block.shape, jnp.int32),
            pltpu.SMEM(lengths.shape, jnp.int32),
            pltpu.VMEM(tokens.shape, tokens.dtype),
            pltpu.VMEM(shift.shape, jnp.float32),
            pltpu.VMEM(scale.shape, jnp.float32),
            pltpu.VMEM(gate.shape, jnp.float32),
            pltpu.VMEM((HEADS, width, 3 * HSIZE), jnp.bfloat16),
            pltpu.VMEM(w_out.shape, jnp.bfloat16),
            pltpu.VMEM((rows, width), jnp.bfloat16),
            pltpu.VMEM((HEADS, rows, 3 * HSIZE), jnp.bfloat16),
            pltpu.VMEM((count, rows, 3 * HSIZE), jnp.bfloat16),
            pltpu.VMEM((slots, rows, HSIZE), jnp.bfloat16),
            pltpu.VMEM((HEADS, rows, HSIZE), jnp.bfloat16),
            pltpu.VMEM((rows, width), jnp.float32),
            pltpu.SMEM((count,), jnp.int32),
            dma((6,)),
            dma((HEADS, 3)),
            dma,
            dma((HEADS, teams)),
            dma((count,)),
            dma((pairs,)),
            dma((slots,)),
            dma((HEADS,)),
        ],
        compiler_params=pltpu.CompilerParams(
            collective_id=0, has_side_effects=True, vmem_limit_bytes=61 * 1024 * 1024
        ),
    )(held_block, lengths, tokens, shift, scale, gate, w_qkv, w_out)


def shards(*args):
    return small(*args) if lax.axis_size("seq") == 16 else large(*args)


def solution(mesh):
    placed = (
        P(("groups", "seq"), None),
        P("groups"),
        P("groups"),
        P("groups", None),
        P("groups", None),
        P("groups", None),
        P(),
        P(),
    )
    return jax.shard_map(
        shards, mesh=mesh, in_specs=placed, out_specs=P(("groups", "seq"), None), check_vma=False
    )
```

```python
import functools
import math

import jax
import jax.numpy as jnp
from jax import lax
from jax.experimental import pallas as pl
from jax.experimental.pallas import tpu as pltpu
from jax.sharding import PartitionSpec as P

HEADS = 6
HSIZE = 128
MESH = pl.DeviceIdType.MESH
NEG = -math.inf
LIMIT = 24


def spread(
    count,
    held_hbm,
    len_hbm,
    tok_hbm,
    shift_hbm,
    scale_hbm,
    gate_hbm,
    w_hbm,
    wo_hbm,
    att_out,
    gate_out,
    part_out,
    held_ref,
    len_ref,
    tok_ref,
    shift_ref,
    scale_ref,
    gate_ref,
    wkv_vm,
    wq_vm,
    wo_vm,
    norm_vm,
    tkv,
    tq,
    rkv,
    rq,
    ao,
    att,
    holder,
    in_sem,
    w_sem,
    wq_sem,
    wo_sem,
    tkv_sem,
    rkv_sem,
    tq_sem,
    rq_sem,
    fwd_sem,
    ao_sem,
    att_sem,
):
    rows, _ = tok_ref.shape
    nvid = len_ref.shape[0]
    pairs = count // 2
    me = lax.axis_index("seq")
    layers = count // 4
    z = me // 4
    y = lax.rem(me // 2, 2)
    core = lax.rem(me, 2)
    low_half = z < layers // 2
    chip = me // 2
    active = jnp.logical_and(chip >= 1, chip <= HEADS)
    my_head = jnp.where(active, chip - 1, 0)
    sibling = chip * 2 + 1 - core
    half = HEADS // 2

    barrier = pltpu.get_barrier_semaphore()

    def head_at(i):
        upper = lax.rem(i // half + jnp.where(low_half, 1, 0), 2)
        k = lax.rem(i, half)
        middle = upper * (half - 1) + 1 + lax.rem(k + y + 1 - core, half - 1)
        return jnp.where(k == 0, upper * (HEADS - 1), middle)

    def load_w(h, part):
        return pltpu.make_async_copy(
            w_hbm.at[:, pl.ds(pl.multiple_of(((part + 1) * HEADS + h) * HSIZE, HSIZE), HSIZE)],
            wkv_vm.at[h, :, pl.ds(part * HSIZE, HSIZE)],
            w_sem.at[h, part],
        )

    loads = [
        pltpu.make_async_copy(src, dst, in_sem.at[i])
        for i, (src, dst) in enumerate(
            (
                (tok_hbm, tok_ref),
                (held_hbm, held_ref),
                (len_hbm, len_ref),
                (shift_hbm, shift_ref),
                (scale_hbm, scale_ref),
                (gate_hbm, gate_ref),
            )
        )
    ]
    for load in loads:
        load.start()
    for part in range(2):
        load_w(head_at(0), part).start()

    def greet(i, _):
        d = lax.rem(me + i, count)
        pl.semaphore_signal(barrier, inc=1, device_id={"seq": d}, device_id_type=MESH)
        return 0

    lax.fori_loop(1, count, greet, 0, unroll=5)

    for i in range(1, HEADS):
        for part in range(2):
            load_w(head_at(i), part).start()
    load_q = pltpu.make_async_copy(w_hbm.at[:, 0 : HEADS * HSIZE], wq_vm, wq_sem)
    load_q.start()
    own = jnp.where(low_half, 0, half)
    load_wo = pltpu.make_async_copy(
        wo_hbm.at[pl.ds(pl.multiple_of(own * HSIZE, HSIZE), half * HSIZE), :], wo_vm, wo_sem
    )
    load_wo.start()

    def span(block):
        video = jnp.int32(0)
        start = jnp.int32(0)
        end = len_ref[0]
        run = len_ref[0]
        for v in range(1, nvid):
            nxt = run + len_ref[v]
            inside = block >= run
            video = jnp.where(inside, v, video)
            start = jnp.where(inside, run, start)
            end = jnp.where(inside, nxt, end)
            run = nxt
        return video, start, end

    loads[0].wait()
    x = tok_ref[...].astype(jnp.float32)
    mean = jnp.mean(x, axis=1, keepdims=True)
    x = x - mean
    var = jnp.mean(x * x, axis=1, keepdims=True)
    x = x * lax.rsqrt(var + 1e-6)
    for load in loads[1:]:
        load.wait()
    my_video, _, _ = span(held_ref[me])
    x = x * (1.0 + scale_ref[pl.ds(my_video, 1), :]) + shift_ref[pl.ds(my_video, 1), :]
    norm_vm[...] = x.astype(jnp.bfloat16)

    def target(h):
        return (h + 1) * 2 + core

    def ship(h, src, dst, send, recv):
        return pltpu.make_async_remote_copy(
            src_ref=src.at[h],
            dst_ref=dst.at[me],
            send_sem=send.at[h],
            recv_sem=recv.at[me],
            device_id={"seq": target(h)},
            device_id_type=MESH,
        )

    def dispatch(h, src, dst, send, recv):
        dest = target(h)

        @pl.when(dest == me)
        def _():
            pltpu.make_async_copy(src.at[h], dst.at[me], recv.at[me]).start()

        @pl.when(dest != me)
        def _():
            ship(h, src, dst, send, recv).start()

    def project(i):
        h = head_at(i)
        for part in range(2):
            load_w(h, part).wait()
        tkv[h] = jnp.dot(norm_vm[...], wkv_vm[h], preferred_element_type=jnp.float32).astype(
            jnp.bfloat16
        )

    def send_kv(i, _):
        project(i)
        dispatch(head_at(i), tkv, rkv, tkv_sem, rkv_sem)
        return 0

    project(0)
    pl.semaphore_wait(barrier, count - 1)
    dispatch(head_at(0), tkv, rkv, tkv_sem, rkv_sem)
    lax.fori_loop(1, HEADS, send_kv, 0)

    load_q.wait()
    queries = jnp.dot(norm_vm[...], wq_vm[...], preferred_element_type=jnp.float32).astype(
        jnp.bfloat16
    )
    for h in range(HEADS):
        tq[h] = queries[:, h * HSIZE : (h + 1) * HSIZE]

    def send_q(i, _):
        dispatch(head_at(i), tq, rq, tq_sem, rq_sem)
        return 0

    lax.fori_loop(0, HEADS, send_q, 0)

    gate_out[...] = gate_ref[pl.ds(my_video, 1), :]

    def find(b, _):
        def look(d, acc):
            return jnp.where(held_ref[d] == b, d, acc)

        holder[b] = lax.fori_loop(0, count, look, jnp.int32(0), unroll=16)
        return 0

    lax.fori_loop(0, count, find, 0)

    def order(i):
        return jnp.where(low_half, pairs - 1 - i, i)

    def forward(t):
        s = t * 2 + core
        return pltpu.make_async_remote_copy(
            src_ref=rkv.at[s],
            dst_ref=rkv.at[s],
            send_sem=fwd_sem.at[t],
            recv_sem=rkv_sem.at[s],
            device_id={"seq": sibling},
            device_id_type=MESH,
        )

    chunk = count // 2
    inv = math.log2(math.e) / math.sqrt(HSIZE)

    def back(t):
        s = t * 2 + core
        return s, pltpu.make_async_remote_copy(
            src_ref=ao.at[t],
            dst_ref=att.at[my_head],
            send_sem=ao_sem.at[t],
            recv_sem=att_sem.at[my_head],
            device_id={"seq": s},
            device_id_type=MESH,
        )

    @pl.when(active)
    def _():
        def relay(i, _):
            t = order(lax.rem(i + pairs // 2, pairs))
            s = t * 2 + core
            pltpu.make_async_copy(rkv.at[s], rkv.at[s], rkv_sem.at[s]).wait()
            forward(t).start()
            return 0

        lax.fori_loop(0, pairs, relay, 0)

        def gather(i, _):
            s = order(lax.rem(i + pairs // 2, pairs)) * 2 + 1 - core
            pltpu.make_async_copy(rkv.at[s], rkv.at[s], rkv_sem.at[s]).wait()
            return 0

        lax.fori_loop(0, pairs, gather, 0)

        def attend(some):
            spans = []
            slots = []
            scores = []
            for t in some:
                s = t * 2 + core
                _, start, end = span(held_ref[s])
                slot = [
                    holder[jnp.maximum(jnp.minimum(start + j, end - 1), 0)] for j in range(chunk)
                ]
                keys = jnp.concatenate([rkv[d, :, 0:HSIZE] for d in slot], axis=0)
                score = lax.dot_general(
                    rq[s], keys, (((1,), (1,)), ((), ())), preferred_element_type=jnp.float32
                )
                spans.append((start, end))
                slots.append(slot)
                scores.append([score[:, j * HSIZE : (j + 1) * HSIZE] for j in range(chunk)])
            tops = [
                jnp.max(functools.reduce(jnp.maximum, score), axis=1, keepdims=True)
                for score in scores
            ]
            weights = [
                [
                    jnp.exp2((score[j] - jnp.where(start + j < end, top, math.inf)) * inv)
                    for j in range(chunk)
                ]
                for score, top, (start, end) in zip(scores, tops, spans)
            ]
            out = []
            for weight, slot in zip(weights, slots):
                values = jnp.concatenate(
                    [rkv[d, :, HSIZE : 2 * HSIZE] for d in slot], axis=0
                )
                weight16 = jnp.concatenate([w.astype(jnp.bfloat16) for w in weight], axis=1)
                summed = jnp.dot(weight16, values, preferred_element_type=jnp.float32)
                total = jnp.sum(functools.reduce(jnp.add, weight), axis=1, keepdims=True)
                out.append((summed / total).astype(jnp.bfloat16))
            return out

        def answer(i, _):
            some = [order(i), jnp.where(low_half, 0, pairs // 2) + i]
            for t in some:
                s = t * 2 + core
                pltpu.make_async_copy(rq.at[s], rq.at[s], rq_sem.at[s]).wait()
            for t, value in zip(some, attend(some)):
                s, copy = back(t)
                ao[t] = value

                @pl.when(s == me)
                def _():
                    pltpu.make_async_copy(ao.at[t], att.at[my_head], att_sem.at[my_head]).start()

                @pl.when(s != me)
                def _():
                    copy.start()

            return 0

        lax.fori_loop(0, pairs // 2, answer, 0)

    def arrived(first):
        for h in range(half):
            part = att.at[first + h]
            pltpu.make_async_copy(part, part, att_sem.at[first + h]).wait()
        return jnp.concatenate([att[first + h] for h in range(half)], axis=1)

    load_wo.wait()
    part_out[...] = jnp.dot(arrived(own), wo_vm[...], preferred_element_type=jnp.float32)
    att_out[...] = arrived(half - own)

    def drain(h, _):
        @pl.when(target(h) != me)
        def _():
            ship(h, tkv, rkv, tkv_sem, rkv_sem).wait_send()
            ship(h, tq, rq, tq_sem, rq_sem).wait_send()

        return 0

    lax.fori_loop(0, HEADS, drain, 0)

    @pl.when(active)
    def _():
        def drain_back(t, _):
            forward(t).wait_send()
            s, copy = back(t)

            @pl.when(s != me)
            def _():
                copy.wait_send()

            return 0

        lax.fori_loop(0, pairs, drain_back, 0)


def finish(count, att_ref, gate_ref, part_ref, wo_ref, out_hbm, out_ref, sem):
    deep = att_ref.shape[1]
    first = jnp.where(lax.axis_index("seq") < count // 2, deep, 0)
    rows = pl.ds(pl.multiple_of(first, deep), deep)
    pieces = sem.shape[0]
    step = out_ref.shape[1] // pieces
    copies = []
    for i in range(pieces):
        cols = pl.ds(i * step, step)
        mixed = jnp.dot(att_ref[...], wo_ref[rows, cols], preferred_element_type=jnp.float32)
        out_ref[:, cols] = ((part_ref[:, cols] + mixed) * gate_ref[:, cols]).astype(out_ref.dtype)
        copies.append(pltpu.make_async_copy(out_ref.at[:, cols], out_hbm.at[:, cols], sem.at[i]))
        copies[-1].start()
    for copy in copies:
        copy.wait()


def small(tokens, held_block, lengths, shift, scale, gate, w_qkv, w_out):
    count = lax.axis_size("seq")
    rows, width = tokens.shape
    pairs = count // 2
    wide = HEADS * HSIZE
    vmem = pl.BlockSpec(memory_space=pltpu.VMEM)
    hbm = pl.BlockSpec(memory_space=pltpu.HBM)
    dma = pltpu.SemaphoreType.DMA
    half = jnp.bfloat16
    pinned = [
        pltpu.with_memory_space_constraint(x, pltpu.HBM)
        for x in (held_block, lengths, tokens, shift, scale, gate, w_qkv, w_out)
    ]
    attended, row, part = pl.pallas_call(
        functools.partial(spread, count),
        out_shape=(
            jax.ShapeDtypeStruct((rows, wide // 2), half),
            jax.ShapeDtypeStruct((1, width), jnp.float32),
            jax.ShapeDtypeStruct((rows, width), jnp.float32),
        ),
        in_specs=[hbm] * 8,
        out_specs=(vmem, vmem, vmem),
        scratch_shapes=[
            pltpu.SMEM(held_block.shape, jnp.int32),
            pltpu.SMEM(lengths.shape, jnp.int32),
            pltpu.VMEM(tokens.shape, tokens.dtype),
            pltpu.VMEM(shift.shape, jnp.float32),
            pltpu.VMEM(scale.shape, jnp.float32),
            pltpu.VMEM(gate.shape, jnp.float32),
            pltpu.VMEM((HEADS, width, 2 * HSIZE), half),
            pltpu.VMEM((width, wide), half),
            pltpu.VMEM((wide // 2, width), half),
            pltpu.VMEM((rows, width), half),
            pltpu.VMEM((HEADS, rows, 2 * HSIZE), half),
            pltpu.VMEM((HEADS, rows, HSIZE), half),
            pltpu.VMEM((count, rows, 2 * HSIZE), half),
            pltpu.VMEM((count, rows, HSIZE), half),
            pltpu.VMEM((pairs, rows, HSIZE), half),
            pltpu.VMEM((HEADS, rows, HSIZE), half),
            pltpu.SMEM((count,), jnp.int32),
            dma((6,)),
            dma((HEADS, 2)),
            dma,
            dma,
            dma((HEADS,)),
            dma((count,)),
            dma((HEADS,)),
            dma((count,)),
            dma((pairs,)),
            dma((pairs,)),
            dma((HEADS,)),
        ],
        compiler_params=pltpu.CompilerParams(
            collective_id=1, has_side_effects=True, vmem_limit_bytes=LIMIT * 1024 * 1024
        ),
    )(*pinned)
    return pl.pallas_call(
        functools.partial(finish, count),
        out_shape=jax.ShapeDtypeStruct((rows, width), half),
        in_specs=[vmem] * 4,
        out_specs=hbm,
        scratch_shapes=[pltpu.VMEM((rows, width), half), dma((3,))],
        compiler_params=pltpu.CompilerParams(vmem_limit_bytes=LIMIT * 1024 * 1024),
    )(attended, row, part, w_out)


def kernel(
    count,
    held_hbm,
    len_hbm,
    tok_hbm,
    shift_hbm,
    scale_hbm,
    gate_hbm,
    w_hbm,
    wo_hbm,
    out_ref,
    held_ref,
    len_ref,
    tok_ref,
    shift_ref,
    scale_ref,
    gate_ref,
    w_vm,
    wo_vm,
    norm_vm,
    tx,
    rx,
    ao,
    att,
    total_ref,
    holder,
    in_sem,
    w_sem,
    wo_sem,
    tx_sem,
    rx_sem,
    fwd_sem,
    ao_sem,
    att_sem,
):
    rows, _ = tok_ref.shape
    nvid = len_ref.shape[0]
    pairs = count // 2
    teams = pairs // HEADS
    shift = (pairs - teams * HEADS) // 2
    me = lax.axis_index("seq")
    chip = me // 2
    core = lax.rem(me, 2)
    sibling = chip * 2 + 1 - core

    barrier = pltpu.get_barrier_semaphore()

    def greet(i, _):
        d = lax.rem(chip + i, pairs) * 2 + core
        pl.semaphore_signal(barrier, inc=1, device_id={"seq": d}, device_id_type=MESH)
        return 0

    lax.fori_loop(1, pairs, greet, 0, unroll=7)
    pl.semaphore_signal(barrier, inc=1, device_id={"seq": sibling}, device_id_type=MESH)

    low_half = chip < pairs // 2

    def head_at(i):
        first = jnp.where(low_half, HEADS // 2, 0) if teams == 1 else 0
        part = HEADS // 2
        return lax.rem(i // part * part + first, HEADS) + lax.rem(i + chip // 2 + chip, part)

    def load_w(h, part):
        return pltpu.make_async_copy(
            w_hbm.at[:, pl.ds(pl.multiple_of((part * HEADS + h) * HSIZE, HSIZE), HSIZE)],
            w_vm.at[h, :, pl.ds(part * HSIZE, HSIZE)],
            w_sem.at[h, part],
        )

    loads = [
        pltpu.make_async_copy(src, dst, in_sem.at[i])
        for i, (src, dst) in enumerate(
            (
                (tok_hbm, tok_ref),
                (held_hbm, held_ref),
                (len_hbm, len_ref),
                (shift_hbm, shift_ref),
                (scale_hbm, scale_ref),
                (gate_hbm, gate_ref),
            )
        )
    ]
    for load in loads:
        load.start()
    for i in range(HEADS // 2):
        for part in range(3):
            load_w(head_at(i), part).start()
    load_wo = pltpu.make_async_copy(wo_hbm, wo_vm, wo_sem)

    def span(block):
        video = jnp.int32(0)
        start = jnp.int32(0)
        end = len_ref[0]
        run = len_ref[0]
        for v in range(1, nvid):
            nxt = run + len_ref[v]
            inside = block >= run
            video = jnp.where(inside, v, video)
            start = jnp.where(inside, run, start)
            end = jnp.where(inside, nxt, end)
            run = nxt
        return video, start, end

    for load in loads:
        load.wait()
    my_video, _, _ = span(held_ref[me])

    x = tok_ref[...].astype(jnp.float32)
    mean = jnp.mean(x, axis=1, keepdims=True)
    x = x - mean
    var = jnp.mean(x * x, axis=1, keepdims=True)
    x = x * lax.rsqrt(var + 1e-6)
    x = x * (1.0 + scale_ref[pl.ds(my_video, 1), :]) + shift_ref[pl.ds(my_video, 1), :]
    norm_vm[...] = x.astype(jnp.bfloat16)

    for i in range(HEADS // 2, HEADS):
        for part in range(3):
            load_w(head_at(i), part).start()
    pl.semaphore_wait(barrier, pairs)

    def ship(h, team):
        dest = (team * HEADS + h + shift) * 2 + core
        return dest, pltpu.make_async_remote_copy(
            src_ref=tx.at[h],
            dst_ref=rx.at[me],
            send_sem=tx_sem.at[h, team],
            recv_sem=rx_sem.at[me],
            device_id={"seq": dest},
            device_id_type=MESH,
        )

    def project(i, _):
        h = head_at(i)
        for part in range(3):
            load_w(h, part).wait()
        tx[h] = jnp.dot(norm_vm[...], w_vm[h], preferred_element_type=jnp.float32).astype(
            jnp.bfloat16
        )

        def send(team, _):
            dest, copy = ship(h, team)

            @pl.when(dest == me)
            def _():
                pltpu.make_async_copy(tx.at[h], rx.at[me], rx_sem.at[me]).start()

            @pl.when(dest != me)
            def _():
                copy.start()

            return 0

        lax.fori_loop(0, teams, send, 0)
        return 0

    lax.fori_loop(0, HEADS, project, 0)

    load_wo.start()

    def find(b, _):
        def look(d, acc):
            return jnp.where(held_ref[d] == b, d, acc)

        holder[b] = lax.fori_loop(0, count, look, jnp.int32(0), unroll=16)
        return 0

    lax.fori_loop(0, count, find, 0)

    active = jnp.logical_and(chip >= shift, chip < teams * HEADS + shift)
    place = jnp.where(active, chip - shift, 0)
    my_head = lax.rem(place, HEADS)
    my_team = place // HEADS
    near = jnp.where(low_half, 0, pairs // 2)
    kv_cols = pl.ds(HSIZE, 2 * HSIZE)

    def forward(s):
        return pltpu.make_async_remote_copy(
            src_ref=rx.at[s, :, kv_cols],
            dst_ref=rx.at[s, :, kv_cols],
            send_sem=fwd_sem.at[s // 2],
            recv_sem=rx_sem.at[s],
            device_id={"seq": sibling},
            device_id_type=MESH,
        )

    key_blocks = count // 2
    chunk = min(8, key_blocks)
    turns = key_blocks // chunk
    mine = pairs if teams == 1 else (pairs - my_team + teams - 1) // teams
    width = 2 if teams == 1 and pairs % 2 == 0 else 1
    inv = math.log2(math.e) / math.sqrt(HSIZE)

    def back(t):
        s = (my_team + t * teams) * 2 + core
        return s, pltpu.make_async_remote_copy(
            src_ref=ao.at[t],
            dst_ref=att.at[my_head],
            send_sem=ao_sem.at[t],
            recv_sem=att_sem.at[my_head],
            device_id={"seq": s},
            device_id_type=MESH,
        )

    @pl.when(active)
    def _():
        def relay(i, _):
            s = lax.rem(i + near, pairs) * 2 + core
            pltpu.make_async_copy(rx.at[s], rx.at[s], rx_sem.at[s]).wait()
            forward(s).start()
            return 0

        lax.fori_loop(0, pairs, relay, 0)

        def gather(i, _):
            s = lax.rem(i + near, pairs) * 2 + 1 - core
            part = rx.at[s, :, kv_cols]
            pltpu.make_async_copy(part, part, rx_sem.at[s]).wait()
            return 0

        lax.fori_loop(0, pairs, gather, 0)

        def attend(t):
            s, _ = back(t)
            _, start, end = span(held_ref[s])
            query = rx[s, :, 0:HSIZE]

            def key_turn(turn, carry):
                top, total, summed = carry
                scores = []
                where = []
                for j in range(chunk):
                    block = start + turn * chunk + j
                    slot = holder[jnp.maximum(jnp.minimum(block, end - 1), 0)]
                    where.append(slot)
                    score = lax.dot_general(
                        query,
                        rx[slot, :, HSIZE : 2 * HSIZE],
                        (((1,), (1,)), ((), ())),
                        preferred_element_type=jnp.float32,
                    )
                    bias = jnp.where(block < end, 0.0, NEG)
                    scores.append(score + bias)
                high = functools.reduce(jnp.maximum, scores)
                new_top = jnp.maximum(top, jnp.max(high, axis=1, keepdims=True))
                factor = jnp.exp2((top - new_top) * inv)
                total = total * factor
                summed = summed * factor
                sums = None
                for j in range(chunk):
                    weight = jnp.exp2((scores[j] - new_top) * inv)
                    sums = weight if sums is None else sums + weight
                    summed = summed + jnp.dot(
                        weight.astype(jnp.bfloat16),
                        rx[where[j], :, 2 * HSIZE : 3 * HSIZE],
                        preferred_element_type=jnp.float32,
                    )
                total = total + jnp.sum(sums, axis=1, keepdims=True)
                return new_top, total, summed

            carry = (
                jnp.full((rows, 1), NEG, jnp.float32),
                jnp.zeros((rows, 1), jnp.float32),
                jnp.zeros((rows, HSIZE), jnp.float32),
            )
            if turns == 1:
                carry = key_turn(0, carry)
            else:
                carry = lax.fori_loop(0, turns, key_turn, carry)
            _, total, summed = carry
            return (summed / total).astype(jnp.bfloat16)

        def answer(i, _):
            some = [
                lax.rem(i * width + u + jnp.where(low_half, mine // 2, 0), mine)
                for u in range(width)
            ]
            for t, value in zip(some, [attend(t) for t in some]):
                s, copy = back(t)
                ao[t] = value

                @pl.when(s == me)
                def _():
                    pltpu.make_async_copy(ao.at[t], att.at[my_head], att_sem.at[my_head]).start()

                @pl.when(s != me)
                def _():
                    copy.start()

            return 0

        lax.fori_loop(0, mine // width, answer, 0)

    load_wo.wait()
    part = HEADS // 2
    first = jnp.where(low_half, 0, part) if teams == 1 else 0

    def mix(first):
        for h in range(part):
            pltpu.make_async_copy(att.at[first + h], att.at[first + h], att_sem.at[first + h]).wait()
        attended = jnp.concatenate([att[first + h] for h in range(part)], axis=1)
        weights = wo_vm[pl.ds(pl.multiple_of(first * HSIZE, HSIZE), part * HSIZE), :]
        return jnp.dot(attended, weights, preferred_element_type=jnp.float32)

    total_ref[...] = mix(first)
    mixed = total_ref[...] + mix(part - first)
    out_ref[...] = (mixed * gate_ref[pl.ds(my_video, 1), :]).astype(out_ref.dtype)

    def drain(i, _):
        h = lax.rem(i, HEADS)
        dest, copy = ship(h, i // HEADS)

        @pl.when(dest != me)
        def _():
            copy.wait_send()

        return 0

    lax.fori_loop(0, HEADS * teams, drain, 0)

    @pl.when(active)
    def _():
        def drain_forward(i, _):
            forward(i * 2 + core).wait_send()
            return 0

        lax.fori_loop(0, pairs, drain_forward, 0)

        def drain_back(t, _):
            s, copy = back(t)

            @pl.when(s != me)
            def _():
                copy.wait_send()

            return 0

        lax.fori_loop(0, mine, drain_back, 0)


def large(tokens, held_block, lengths, shift, scale, gate, w_qkv, w_out):
    count = lax.axis_size("seq")
    rows, width = tokens.shape
    pairs = count // 2
    teams = pairs // HEADS
    slots = -(-pairs // teams)
    vmem = pl.BlockSpec(memory_space=pltpu.VMEM)
    hbm = pl.BlockSpec(memory_space=pltpu.HBM)
    dma = pltpu.SemaphoreType.DMA
    return pl.pallas_call(
        functools.partial(kernel, count),
        out_shape=jax.ShapeDtypeStruct((rows, width), jnp.bfloat16),
        in_specs=[hbm] * 8,
        out_specs=vmem,
        scratch_shapes=[
            pltpu.SMEM(held_block.shape, jnp.int32),
            pltpu.SMEM(lengths.shape, jnp.int32),
            pltpu.VMEM(tokens.shape, tokens.dtype),
            pltpu.VMEM(shift.shape, jnp.float32),
            pltpu.VMEM(scale.shape, jnp.float32),
            pltpu.VMEM(gate.shape, jnp.float32),
            pltpu.VMEM((HEADS, width, 3 * HSIZE), jnp.bfloat16),
            pltpu.VMEM(w_out.shape, jnp.bfloat16),
            pltpu.VMEM((rows, width), jnp.bfloat16),
            pltpu.VMEM((HEADS, rows, 3 * HSIZE), jnp.bfloat16),
            pltpu.VMEM((count, rows, 3 * HSIZE), jnp.bfloat16),
            pltpu.VMEM((slots, rows, HSIZE), jnp.bfloat16),
            pltpu.VMEM((HEADS, rows, HSIZE), jnp.bfloat16),
            pltpu.VMEM((rows, width), jnp.float32),
            pltpu.SMEM((count,), jnp.int32),
            dma((6,)),
            dma((HEADS, 3)),
            dma,
            dma((HEADS, teams)),
            dma((count,)),
            dma((pairs,)),
            dma((slots,)),
            dma((HEADS,)),
        ],
        compiler_params=pltpu.CompilerParams(
            collective_id=0, has_side_effects=True, vmem_limit_bytes=61 * 1024 * 1024
        ),
    )(held_block, lengths, tokens, shift, scale, gate, w_qkv, w_out)


def shards(*args):
    return small(*args) if lax.axis_size("seq") == 16 else large(*args)


def solution(mesh):
    placed = (
        P(("groups", "seq"), None),
        P("groups"),
        P("groups"),
        P("groups", None),
        P("groups", None),
        P("groups", None),
        P(),
        P(),
    )
    return jax.shard_map(
        shards, mesh=mesh, in_specs=placed, out_specs=P(("groups", "seq"), None), check_vma=False
    )
```

```python
import functools
import math

import jax
import jax.numpy as jnp
from jax import lax
from jax.experimental import pallas as pl
from jax.experimental.pallas import tpu as pltpu
from jax.sharding import PartitionSpec as P

HEADS = 6
HSIZE = 128
MESH = pl.DeviceIdType.MESH
NEG = -math.inf
LIMIT = 24


def spread(
    count,
    held_hbm,
    len_hbm,
    tok_hbm,
    shift_hbm,
    scale_hbm,
    gate_hbm,
    w_hbm,
    wo_hbm,
    att_out,
    gate_out,
    part_out,
    held_ref,
    len_ref,
    tok_ref,
    shift_ref,
    scale_ref,
    gate_ref,
    wkv_vm,
    wq_vm,
    wo_vm,
    norm_vm,
    tkv,
    tq,
    rkv,
    rq,
    ao,
    att,
    holder,
    in_sem,
    w_sem,
    wq_sem,
    wo_sem,
    tkv_sem,
    rkv_sem,
    tq_sem,
    rq_sem,
    fwd_sem,
    ao_sem,
    att_sem,
):
    rows, _ = tok_ref.shape
    nvid = len_ref.shape[0]
    pairs = count // 2
    me = lax.axis_index("seq")
    layers = count // 4
    z = me // 4
    y = lax.rem(me // 2, 2)
    core = lax.rem(me, 2)
    low_half = z < layers // 2
    chip = me // 2
    active = jnp.logical_and(chip >= 1, chip <= HEADS)
    my_head = jnp.where(active, chip - 1, 0)
    sibling = chip * 2 + 1 - core
    half = HEADS // 2

    barrier = pltpu.get_barrier_semaphore()

    def head_at(i):
        upper = lax.rem(i // half + jnp.where(low_half, 1, 0), 2)
        k = lax.rem(i, half)
        middle = upper * (half - 1) + 1 + lax.rem(k + y + 1 - core, half - 1)
        return jnp.where(k == 0, upper * (HEADS - 1), middle)

    def load_w(h, part):
        return pltpu.make_async_copy(
            w_hbm.at[:, pl.ds(pl.multiple_of(((part + 1) * HEADS + h) * HSIZE, HSIZE), HSIZE)],
            wkv_vm.at[h, :, pl.ds(part * HSIZE, HSIZE)],
            w_sem.at[h, part],
        )

    loads = [
        pltpu.make_async_copy(src, dst, in_sem.at[i])
        for i, (src, dst) in enumerate(
            (
                (tok_hbm, tok_ref),
                (held_hbm, held_ref),
                (len_hbm, len_ref),
                (shift_hbm, shift_ref),
                (scale_hbm, scale_ref),
                (gate_hbm, gate_ref),
            )
        )
    ]
    for load in loads:
        load.start()
    for part in range(2):
        load_w(head_at(0), part).start()

    def greet(i, _):
        d = lax.rem(me + i, count)
        pl.semaphore_signal(barrier, inc=1, device_id={"seq": d}, device_id_type=MESH)
        return 0

    lax.fori_loop(1, count, greet, 0, unroll=5)

    for i in range(1, HEADS):
        for part in range(2):
            load_w(head_at(i), part).start()
    load_q = pltpu.make_async_copy(w_hbm.at[:, 0 : HEADS * HSIZE], wq_vm, wq_sem)
    load_q.start()
    own = jnp.where(low_half, 0, half)
    load_wo = pltpu.make_async_copy(
        wo_hbm.at[pl.ds(pl.multiple_of(own * HSIZE, HSIZE), half * HSIZE), :], wo_vm, wo_sem
    )
    load_wo.start()

    def span(block):
        video = jnp.int32(0)
        start = jnp.int32(0)
        end = len_ref[0]
        run = len_ref[0]
        for v in range(1, nvid):
            nxt = run + len_ref[v]
            inside = block >= run
            video = jnp.where(inside, v, video)
            start = jnp.where(inside, run, start)
            end = jnp.where(inside, nxt, end)
            run = nxt
        return video, start, end

    loads[0].wait()
    x = tok_ref[...].astype(jnp.float32)
    mean = jnp.mean(x, axis=1, keepdims=True)
    x = x - mean
    var = jnp.mean(x * x, axis=1, keepdims=True)
    x = x * lax.rsqrt(var + 1e-6)
    for load in loads[1:]:
        load.wait()
    my_video, _, _ = span(held_ref[me])
    x = x * (1.0 + scale_ref[pl.ds(my_video, 1), :]) + shift_ref[pl.ds(my_video, 1), :]
    norm_vm[...] = x.astype(jnp.bfloat16)

    def target(h):
        return (h + 1) * 2 + core

    def ship(h, src, dst, send, recv):
        return pltpu.make_async_remote_copy(
            src_ref=src.at[h],
            dst_ref=dst.at[me],
            send_sem=send.at[h],
            recv_sem=recv.at[me],
            device_id={"seq": target(h)},
            device_id_type=MESH,
        )

    def dispatch(h, src, dst, send, recv):
        dest = target(h)

        @pl.when(dest == me)
        def _():
            pltpu.make_async_copy(src.at[h], dst.at[me], recv.at[me]).start()

        @pl.when(dest != me)
        def _():
            ship(h, src, dst, send, recv).start()

    def project(i):
        h = head_at(i)
        for part in range(2):
            load_w(h, part).wait()
        tkv[h] = jnp.dot(norm_vm[...], wkv_vm[h], preferred_element_type=jnp.float32).astype(
            jnp.bfloat16
        )

    def send_kv(i, _):
        project(i)
        dispatch(head_at(i), tkv, rkv, tkv_sem, rkv_sem)
        return 0

    project(0)
    pl.semaphore_wait(barrier, count - 1)
    dispatch(head_at(0), tkv, rkv, tkv_sem, rkv_sem)
    lax.fori_loop(1, HEADS, send_kv, 0)

    load_q.wait()
    queries = jnp.dot(norm_vm[...], wq_vm[...], preferred_element_type=jnp.float32).astype(
        jnp.bfloat16
    )
    for h in range(HEADS):
        tq[h] = queries[:, h * HSIZE : (h + 1) * HSIZE]

    def send_q(i, _):
        dispatch(head_at(i), tq, rq, tq_sem, rq_sem)
        return 0

    lax.fori_loop(0, HEADS, send_q, 0)

    gate_out[...] = gate_ref[pl.ds(my_video, 1), :]

    def find(b, _):
        def look(d, acc):
            return jnp.where(held_ref[d] == b, d, acc)

        holder[b] = lax.fori_loop(0, count, look, jnp.int32(0), unroll=16)
        return 0

    lax.fori_loop(0, count, find, 0)

    def order(i):
        return jnp.where(low_half, pairs - 1 - i, i)

    def forward(t):
        s = t * 2 + core
        return pltpu.make_async_remote_copy(
            src_ref=rkv.at[s],
            dst_ref=rkv.at[s],
            send_sem=fwd_sem.at[t],
            recv_sem=rkv_sem.at[s],
            device_id={"seq": sibling},
            device_id_type=MESH,
        )

    chunk = count // 2
    inv = math.log2(math.e) / math.sqrt(HSIZE)

    def back(t):
        s = t * 2 + core
        return s, pltpu.make_async_remote_copy(
            src_ref=ao.at[t],
            dst_ref=att.at[my_head],
            send_sem=ao_sem.at[t],
            recv_sem=att_sem.at[my_head],
            device_id={"seq": s},
            device_id_type=MESH,
        )

    @pl.when(active)
    def _():
        def relay(i, _):
            t = order(lax.rem(i + pairs // 2, pairs))
            s = t * 2 + core
            pltpu.make_async_copy(rkv.at[s], rkv.at[s], rkv_sem.at[s]).wait()
            forward(t).start()
            return 0

        lax.fori_loop(0, pairs, relay, 0)

        def gather(i, _):
            s = order(lax.rem(i + pairs // 2, pairs)) * 2 + 1 - core
            pltpu.make_async_copy(rkv.at[s], rkv.at[s], rkv_sem.at[s]).wait()
            return 0

        lax.fori_loop(0, pairs, gather, 0)

        def attend(some):
            spans = []
            slots = []
            scores = []
            for t in some:
                s = t * 2 + core
                _, start, end = span(held_ref[s])
                slot = [
                    holder[jnp.maximum(jnp.minimum(start + j, end - 1), 0)] for j in range(chunk)
                ]
                keys = jnp.concatenate([rkv[d, :, 0:HSIZE] for d in slot], axis=0)
                score = lax.dot_general(
                    rq[s], keys, (((1,), (1,)), ((), ())), preferred_element_type=jnp.float32
                )
                spans.append((start, end))
                slots.append(slot)
                scores.append([score[:, j * HSIZE : (j + 1) * HSIZE] for j in range(chunk)])
            tops = [
                jnp.max(functools.reduce(jnp.maximum, score), axis=1, keepdims=True)
                for score in scores
            ]
            weights = [
                [
                    jnp.exp2((score[j] - jnp.where(start + j < end, top, math.inf)) * inv)
                    for j in range(chunk)
                ]
                for score, top, (start, end) in zip(scores, tops, spans)
            ]
            out = []
            for weight, slot in zip(weights, slots):
                values = jnp.concatenate(
                    [rkv[d, :, HSIZE : 2 * HSIZE] for d in slot], axis=0
                )
                weight16 = jnp.concatenate([w.astype(jnp.bfloat16) for w in weight], axis=1)
                summed = jnp.dot(weight16, values, preferred_element_type=jnp.float32)
                total = jnp.sum(functools.reduce(jnp.add, weight), axis=1, keepdims=True)
                out.append((summed / total).astype(jnp.bfloat16))
            return out

        def answer(i, _):
            some = [order(i), jnp.where(low_half, 0, pairs // 2) + i]
            for t in some:
                s = t * 2 + core
                pltpu.make_async_copy(rq.at[s], rq.at[s], rq_sem.at[s]).wait()
            for t, value in zip(some, attend(some)):
                s, copy = back(t)
                ao[t] = value

                @pl.when(s == me)
                def _():
                    pltpu.make_async_copy(ao.at[t], att.at[my_head], att_sem.at[my_head]).start()

                @pl.when(s != me)
                def _():
                    copy.start()

            return 0

        lax.fori_loop(0, pairs // 2, answer, 0)

    def drain(h, _):
        @pl.when(target(h) != me)
        def _():
            ship(h, tkv, rkv, tkv_sem, rkv_sem).wait_send()
            ship(h, tq, rq, tq_sem, rq_sem).wait_send()

        return 0

    lax.fori_loop(0, HEADS, drain, 0)

    def arrived(first):
        for h in range(half):
            part = att.at[first + h]
            pltpu.make_async_copy(part, part, att_sem.at[first + h]).wait()
        return jnp.concatenate([att[first + h] for h in range(half)], axis=1)

    load_wo.wait()
    part_out[...] = jnp.dot(arrived(own), wo_vm[...], preferred_element_type=jnp.float32)

    @pl.when(active)
    def _():
        def drain_back(t, _):
            forward(t).wait_send()
            s, copy = back(t)

            @pl.when(s != me)
            def _():
                copy.wait_send()

            return 0

        lax.fori_loop(0, pairs, drain_back, 0)

    att_out[...] = arrived(half - own)


def finish(count, att_ref, gate_ref, part_ref, wo_ref, out_hbm, out_ref, sem):
    deep = att_ref.shape[1]
    first = jnp.where(lax.axis_index("seq") < count // 2, deep, 0)
    rows = pl.ds(pl.multiple_of(first, deep), deep)
    pieces = sem.shape[0]
    step = out_ref.shape[1] // pieces
    copies = []
    for i in range(pieces):
        cols = pl.ds(i * step, step)
        mixed = jnp.dot(att_ref[...], wo_ref[rows, cols], preferred_element_type=jnp.float32)
        out_ref[:, cols] = ((part_ref[:, cols] + mixed) * gate_ref[:, cols]).astype(out_ref.dtype)
        copies.append(pltpu.make_async_copy(out_ref.at[:, cols], out_hbm.at[:, cols], sem.at[i]))
        copies[-1].start()
    for copy in copies:
        copy.wait()


def small(tokens, held_block, lengths, shift, scale, gate, w_qkv, w_out):
    count = lax.axis_size("seq")
    rows, width = tokens.shape
    pairs = count // 2
    wide = HEADS * HSIZE
    vmem = pl.BlockSpec(memory_space=pltpu.VMEM)
    hbm = pl.BlockSpec(memory_space=pltpu.HBM)
    dma = pltpu.SemaphoreType.DMA
    half = jnp.bfloat16
    pinned = [
        pltpu.with_memory_space_constraint(x, pltpu.HBM)
        for x in (held_block, lengths, tokens, shift, scale, gate, w_qkv, w_out)
    ]
    attended, row, part = pl.pallas_call(
        functools.partial(spread, count),
        out_shape=(
            jax.ShapeDtypeStruct((rows, wide // 2), half),
            jax.ShapeDtypeStruct((1, width), jnp.float32),
            jax.ShapeDtypeStruct((rows, width), jnp.float32),
        ),
        in_specs=[hbm] * 8,
        out_specs=(vmem, vmem, vmem),
        scratch_shapes=[
            pltpu.SMEM(held_block.shape, jnp.int32),
            pltpu.SMEM(lengths.shape, jnp.int32),
            pltpu.VMEM(tokens.shape, tokens.dtype),
            pltpu.VMEM(shift.shape, jnp.float32),
            pltpu.VMEM(scale.shape, jnp.float32),
            pltpu.VMEM(gate.shape, jnp.float32),
            pltpu.VMEM((HEADS, width, 2 * HSIZE), half),
            pltpu.VMEM((width, wide), half),
            pltpu.VMEM((wide // 2, width), half),
            pltpu.VMEM((rows, width), half),
            pltpu.VMEM((HEADS, rows, 2 * HSIZE), half),
            pltpu.VMEM((HEADS, rows, HSIZE), half),
            pltpu.VMEM((count, rows, 2 * HSIZE), half),
            pltpu.VMEM((count, rows, HSIZE), half),
            pltpu.VMEM((pairs, rows, HSIZE), half),
            pltpu.VMEM((HEADS, rows, HSIZE), half),
            pltpu.SMEM((count,), jnp.int32),
            dma((6,)),
            dma((HEADS, 2)),
            dma,
            dma,
            dma((HEADS,)),
            dma((count,)),
            dma((HEADS,)),
            dma((count,)),
            dma((pairs,)),
            dma((pairs,)),
            dma((HEADS,)),
        ],
        compiler_params=pltpu.CompilerParams(
            collective_id=1, has_side_effects=True, vmem_limit_bytes=LIMIT * 1024 * 1024
        ),
    )(*pinned)
    return pl.pallas_call(
        functools.partial(finish, count),
        out_shape=jax.ShapeDtypeStruct((rows, width), half),
        in_specs=[vmem] * 4,
        out_specs=hbm,
        scratch_shapes=[pltpu.VMEM((rows, width), half), dma((3,))],
        compiler_params=pltpu.CompilerParams(vmem_limit_bytes=LIMIT * 1024 * 1024),
    )(attended, row, part, w_out)


def kernel(
    count,
    held_hbm,
    len_hbm,
    tok_hbm,
    shift_hbm,
    scale_hbm,
    gate_hbm,
    w_hbm,
    wo_hbm,
    out_ref,
    held_ref,
    len_ref,
    tok_ref,
    shift_ref,
    scale_ref,
    gate_ref,
    w_vm,
    wo_vm,
    norm_vm,
    tx,
    rx,
    ao,
    att,
    total_ref,
    holder,
    in_sem,
    w_sem,
    wo_sem,
    tx_sem,
    rx_sem,
    fwd_sem,
    ao_sem,
    att_sem,
):
    rows, _ = tok_ref.shape
    nvid = len_ref.shape[0]
    pairs = count // 2
    teams = pairs // HEADS
    shift = (pairs - teams * HEADS) // 2
    me = lax.axis_index("seq")
    chip = me // 2
    core = lax.rem(me, 2)
    sibling = chip * 2 + 1 - core

    barrier = pltpu.get_barrier_semaphore()

    def greet(i, _):
        d = lax.rem(chip + i, pairs) * 2 + core
        pl.semaphore_signal(barrier, inc=1, device_id={"seq": d}, device_id_type=MESH)
        return 0

    lax.fori_loop(1, pairs, greet, 0, unroll=7)
    pl.semaphore_signal(barrier, inc=1, device_id={"seq": sibling}, device_id_type=MESH)

    low_half = chip < pairs // 2

    def head_at(i):
        first = jnp.where(low_half, HEADS // 2, 0) if teams == 1 else 0
        part = HEADS // 2
        return lax.rem(i // part * part + first, HEADS) + lax.rem(i + chip // 2 + chip, part)

    def load_w(h, part):
        return pltpu.make_async_copy(
            w_hbm.at[:, pl.ds(pl.multiple_of((part * HEADS + h) * HSIZE, HSIZE), HSIZE)],
            w_vm.at[h, :, pl.ds(part * HSIZE, HSIZE)],
            w_sem.at[h, part],
        )

    loads = [
        pltpu.make_async_copy(src, dst, in_sem.at[i])
        for i, (src, dst) in enumerate(
            (
                (tok_hbm, tok_ref),
                (held_hbm, held_ref),
                (len_hbm, len_ref),
                (shift_hbm, shift_ref),
                (scale_hbm, scale_ref),
                (gate_hbm, gate_ref),
            )
        )
    ]
    for load in loads:
        load.start()
    for i in range(HEADS // 2):
        for part in range(3):
            load_w(head_at(i), part).start()
    load_wo = pltpu.make_async_copy(wo_hbm, wo_vm, wo_sem)

    def span(block):
        video = jnp.int32(0)
        start = jnp.int32(0)
        end = len_ref[0]
        run = len_ref[0]
        for v in range(1, nvid):
            nxt = run + len_ref[v]
            inside = block >= run
            video = jnp.where(inside, v, video)
            start = jnp.where(inside, run, start)
            end = jnp.where(inside, nxt, end)
            run = nxt
        return video, start, end

    for load in loads:
        load.wait()
    my_video, _, _ = span(held_ref[me])

    x = tok_ref[...].astype(jnp.float32)
    mean = jnp.mean(x, axis=1, keepdims=True)
    x = x - mean
    var = jnp.mean(x * x, axis=1, keepdims=True)
    x = x * lax.rsqrt(var + 1e-6)
    x = x * (1.0 + scale_ref[pl.ds(my_video, 1), :]) + shift_ref[pl.ds(my_video, 1), :]
    norm_vm[...] = x.astype(jnp.bfloat16)

    for i in range(HEADS // 2, HEADS):
        for part in range(3):
            load_w(head_at(i), part).start()
    pl.semaphore_wait(barrier, pairs)

    def ship(h, team):
        dest = (team * HEADS + h + shift) * 2 + core
        return dest, pltpu.make_async_remote_copy(
            src_ref=tx.at[h],
            dst_ref=rx.at[me],
            send_sem=tx_sem.at[h, team],
            recv_sem=rx_sem.at[me],
            device_id={"seq": dest},
            device_id_type=MESH,
        )

    def project(i, _):
        h = head_at(i)
        for part in range(3):
            load_w(h, part).wait()
        tx[h] = jnp.dot(norm_vm[...], w_vm[h], preferred_element_type=jnp.float32).astype(
            jnp.bfloat16
        )

        def send(team, _):
            dest, copy = ship(h, team)

            @pl.when(dest == me)
            def _():
                pltpu.make_async_copy(tx.at[h], rx.at[me], rx_sem.at[me]).start()

            @pl.when(dest != me)
            def _():
                copy.start()

            return 0

        lax.fori_loop(0, teams, send, 0)
        return 0

    lax.fori_loop(0, HEADS, project, 0)

    load_wo.start()

    def find(b, _):
        def look(d, acc):
            return jnp.where(held_ref[d] == b, d, acc)

        holder[b] = lax.fori_loop(0, count, look, jnp.int32(0), unroll=16)
        return 0

    lax.fori_loop(0, count, find, 0)

    active = jnp.logical_and(chip >= shift, chip < teams * HEADS + shift)
    place = jnp.where(active, chip - shift, 0)
    my_head = lax.rem(place, HEADS)
    my_team = place // HEADS
    near = jnp.where(low_half, 0, pairs // 2)
    kv_cols = pl.ds(HSIZE, 2 * HSIZE)

    def forward(s):
        return pltpu.make_async_remote_copy(
            src_ref=rx.at[s, :, kv_cols],
            dst_ref=rx.at[s, :, kv_cols],
            send_sem=fwd_sem.at[s // 2],
            recv_sem=rx_sem.at[s],
            device_id={"seq": sibling},
            device_id_type=MESH,
        )

    key_blocks = count // 2
    chunk = min(8, key_blocks)
    turns = key_blocks // chunk
    mine = pairs if teams == 1 else (pairs - my_team + teams - 1) // teams
    width = 2 if teams == 1 and pairs % 2 == 0 else 1
    inv = math.log2(math.e) / math.sqrt(HSIZE)

    def back(t):
        s = (my_team + t * teams) * 2 + core
        return s, pltpu.make_async_remote_copy(
            src_ref=ao.at[t],
            dst_ref=att.at[my_head],
            send_sem=ao_sem.at[t],
            recv_sem=att_sem.at[my_head],
            device_id={"seq": s},
            device_id_type=MESH,
        )

    @pl.when(active)
    def _():
        def relay(i, _):
            s = lax.rem(i + near, pairs) * 2 + core
            pltpu.make_async_copy(rx.at[s], rx.at[s], rx_sem.at[s]).wait()
            forward(s).start()
            return 0

        lax.fori_loop(0, pairs, relay, 0)

        def gather(i, _):
            s = lax.rem(i + near, pairs) * 2 + 1 - core
            part = rx.at[s, :, kv_cols]
            pltpu.make_async_copy(part, part, rx_sem.at[s]).wait()
            return 0

        lax.fori_loop(0, pairs, gather, 0)

        def attend(t):
            s, _ = back(t)
            _, start, end = span(held_ref[s])
            query = rx[s, :, 0:HSIZE]

            def key_turn(turn, carry):
                top, total, summed = carry
                scores = []
                where = []
                for j in range(chunk):
                    block = start + turn * chunk + j
                    slot = holder[jnp.maximum(jnp.minimum(block, end - 1), 0)]
                    where.append(slot)
                    score = lax.dot_general(
                        query,
                        rx[slot, :, HSIZE : 2 * HSIZE],
                        (((1,), (1,)), ((), ())),
                        preferred_element_type=jnp.float32,
                    )
                    bias = jnp.where(block < end, 0.0, NEG)
                    scores.append(score + bias)
                high = functools.reduce(jnp.maximum, scores)
                new_top = jnp.maximum(top, jnp.max(high, axis=1, keepdims=True))
                factor = jnp.exp2((top - new_top) * inv)
                total = total * factor
                summed = summed * factor
                sums = None
                for j in range(chunk):
                    weight = jnp.exp2((scores[j] - new_top) * inv)
                    sums = weight if sums is None else sums + weight
                    summed = summed + jnp.dot(
                        weight.astype(jnp.bfloat16),
                        rx[where[j], :, 2 * HSIZE : 3 * HSIZE],
                        preferred_element_type=jnp.float32,
                    )
                total = total + jnp.sum(sums, axis=1, keepdims=True)
                return new_top, total, summed

            carry = (
                jnp.full((rows, 1), NEG, jnp.float32),
                jnp.zeros((rows, 1), jnp.float32),
                jnp.zeros((rows, HSIZE), jnp.float32),
            )
            if turns == 1:
                carry = key_turn(0, carry)
            else:
                carry = lax.fori_loop(0, turns, key_turn, carry)
            _, total, summed = carry
            return (summed / total).astype(jnp.bfloat16)

        def answer(i, _):
            some = [
                lax.rem(i * width + u + jnp.where(low_half, mine // 2, 0), mine)
                for u in range(width)
            ]
            for t, value in zip(some, [attend(t) for t in some]):
                s, copy = back(t)
                ao[t] = value

                @pl.when(s == me)
                def _():
                    pltpu.make_async_copy(ao.at[t], att.at[my_head], att_sem.at[my_head]).start()

                @pl.when(s != me)
                def _():
                    copy.start()

            return 0

        lax.fori_loop(0, mine // width, answer, 0)

    load_wo.wait()
    part = HEADS // 2
    first = jnp.where(low_half, 0, part) if teams == 1 else 0

    def mix(first):
        for h in range(part):
            pltpu.make_async_copy(att.at[first + h], att.at[first + h], att_sem.at[first + h]).wait()
        attended = jnp.concatenate([att[first + h] for h in range(part)], axis=1)
        weights = wo_vm[pl.ds(pl.multiple_of(first * HSIZE, HSIZE), part * HSIZE), :]
        return jnp.dot(attended, weights, preferred_element_type=jnp.float32)

    total_ref[...] = mix(first)
    mixed = total_ref[...] + mix(part - first)
    out_ref[...] = (mixed * gate_ref[pl.ds(my_video, 1), :]).astype(out_ref.dtype)

    def drain(i, _):
        h = lax.rem(i, HEADS)
        dest, copy = ship(h, i // HEADS)

        @pl.when(dest != me)
        def _():
            copy.wait_send()

        return 0

    lax.fori_loop(0, HEADS * teams, drain, 0)

    @pl.when(active)
    def _():
        def drain_forward(i, _):
            forward(i * 2 + core).wait_send()
            return 0

        lax.fori_loop(0, pairs, drain_forward, 0)

        def drain_back(t, _):
            s, copy = back(t)

            @pl.when(s != me)
            def _():
                copy.wait_send()

            return 0

        lax.fori_loop(0, mine, drain_back, 0)


def large(tokens, held_block, lengths, shift, scale, gate, w_qkv, w_out):
    count = lax.axis_size("seq")
    rows, width = tokens.shape
    pairs = count // 2
    teams = pairs // HEADS
    slots = -(-pairs // teams)
    vmem = pl.BlockSpec(memory_space=pltpu.VMEM)
    hbm = pl.BlockSpec(memory_space=pltpu.HBM)
    dma = pltpu.SemaphoreType.DMA
    return pl.pallas_call(
        functools.partial(kernel, count),
        out_shape=jax.ShapeDtypeStruct((rows, width), jnp.bfloat16),
        in_specs=[hbm] * 8,
        out_specs=vmem,
        scratch_shapes=[
            pltpu.SMEM(held_block.shape, jnp.int32),
            pltpu.SMEM(lengths.shape, jnp.int32),
            pltpu.VMEM(tokens.shape, tokens.dtype),
            pltpu.VMEM(shift.shape, jnp.float32),
            pltpu.VMEM(scale.shape, jnp.float32),
            pltpu.VMEM(gate.shape, jnp.float32),
            pltpu.VMEM((HEADS, width, 3 * HSIZE), jnp.bfloat16),
            pltpu.VMEM(w_out.shape, jnp.bfloat16),
            pltpu.VMEM((rows, width), jnp.bfloat16),
            pltpu.VMEM((HEADS, rows, 3 * HSIZE), jnp.bfloat16),
            pltpu.VMEM((count, rows, 3 * HSIZE), jnp.bfloat16),
            pltpu.VMEM((slots, rows, HSIZE), jnp.bfloat16),
            pltpu.VMEM((HEADS, rows, HSIZE), jnp.bfloat16),
            pltpu.VMEM((rows, width), jnp.float32),
            pltpu.SMEM((count,), jnp.int32),
            dma((6,)),
            dma((HEADS, 3)),
            dma,
            dma((HEADS, teams)),
            dma((count,)),
            dma((pairs,)),
            dma((slots,)),
            dma((HEADS,)),
        ],
        compiler_params=pltpu.CompilerParams(
            collective_id=0, has_side_effects=True, vmem_limit_bytes=61 * 1024 * 1024
        ),
    )(held_block, lengths, tokens, shift, scale, gate, w_qkv, w_out)


def shards(*args):
    return small(*args) if lax.axis_size("seq") == 16 else large(*args)


def solution(mesh):
    placed = (
        P(("groups", "seq"), None),
        P("groups"),
        P("groups"),
        P("groups", None),
        P("groups", None),
        P("groups", None),
        P(),
        P(),
    )
    return jax.shard_map(
        shards, mesh=mesh, in_specs=placed, out_specs=P(("groups", "seq"), None), check_vma=False
    )
```
